128 devices in a mesh: dp: 32 (over y, x, core), mp: 4 (over z).
Axes of the slice: x: 4, y: 4, z: 4, core: 2. Of those that a mesh axis runs over, the one named last changes fastest.
Arguments:
- query_hidden: bfloat16 [16384, 4096], P('dp'), may hold values from -6 to 6
- passage_hidden: bfloat16 [16384, 4096], P('dp'), may hold values from -6 to 6
- head_weight: bfloat16 [4096, 4096], P(None, 'mp'), may hold values from -0.09375 to 0.09375
- neg_blocks: int32 [128, 4], P('dp'), may hold values from 0 to 127, as said below
- pos_ids: int32 [16384], P('dp'), may hold values from 0 to 127
Outputs:
- query_loss: float32 [16384], P('dp')
- grad_weight: float32 [4096, 4096], P('dp', 'mp')
- grad_query_hidden: bfloat16 [16384, 4096], P('dp', 'mp')
- grad_passage_hidden: bfloat16 [16384, 4096], P('dp', 'mp')
The draws below stay inside these ranges and needn't reach their ends.
Inputs may be any that keep to these rules, and one draw needn't show every extreme that they name: `neg_blocks`: within each aligned group of 4 query blocks all 16 ids are different, and at most 1 of them fall into any one aligned group of 4 passage block ids; some group of passage blocks receives exactly 1 of them.
All inputs are finite; a program needn't handle non-finite values.
Results may differ from the reference program's by a relative error of at most 0.017.
Values may be sent and summed in bfloat16 or wider, within the bound.
A program may use at most 128 MiB of HBM per device.

```python
import jax
import jax.numpy as jnp
from jax import lax

D = 4096
BLK = 128
K = 4
QB_DEV = 4
NQB = 128
NQ = 16384
CAP = 1
N_MP = 4


def draw_neg_blocks(key, part):
    device_count = NQB // QB_DEV
    slot_count = device_count * CAP
    request_count = QB_DEV * K
    first_key = jax.random.fold_in(key, 11)
    second_key = jax.random.fold_in(key, 23)
    ranking = jax.random.randint(first_key, (device_count, slot_count), 0, 1048576, dtype=jnp.int32)
    ranking = ranking * slot_count + jnp.arange(slot_count, dtype=jnp.int32)[None, :]
    chosen_slots = jnp.argsort(ranking, axis=1, stable=True)[:, :request_count].astype(jnp.int32)
    owners = chosen_slots // CAP
    within = chosen_slots % CAP
    offsets = jax.random.randint(second_key, (device_count, device_count), 0, QB_DEV, dtype=jnp.int32)
    base_local = jnp.take_along_axis(offsets, owners, axis=1)
    local_ids = (base_local + within) % QB_DEV
    block_ids = owners * QB_DEV + local_ids
    return block_ids.reshape(NQB, K).astype(jnp.int32)


def place_ends(result, key, low, high):
    longest = result.shape.index(max(result.shape))
    spots = []
    for shift in (0, 1):
        where = [jax.random.randint(jax.random.fold_in(key, axis), (), 0, length) for axis, length in enumerate(result.shape)]
        where[longest] = (where[longest] + shift) % result.shape[longest]
        spots.append(tuple(where))
    return result.at[spots[0]].set(low).at[spots[1]].set(high)


def spiked(drawn, own_key, source, target, blocks, factor):
    def block_of(axis_at):
        return (jnp.arange(drawn.shape[axis_at]) // (drawn.shape[axis_at] // blocks)).reshape((-1,) + (1,) * (drawn.ndim - 1 - axis_at))

    one_side = jax.random.permutation(own_key, blocks)[block_of(target)]
    second = (block_of(target) + blocks // 2) % blocks
    return jnp.where((block_of(source) == one_side) | (block_of(source) == second), factor * drawn, drawn)


def levels(stream_key, dims, cuts, smallest, largest):
    def one(dim, shards_of):
        heights = jax.random.uniform(jax.random.fold_in(jax.random.fold_in(stream_key, 6), dim), (shards_of,), jnp.float32, smallest / len(cuts), largest / len(cuts))
        return jnp.repeat(jnp.exp(heights), dims[dim] // shards_of).reshape((-1,) + (1,) * (len(dims) - dim - 1))

    level = one(*cuts[0])
    for cut in cuts[1:]:
        level = level * one(*cut)
    return level


def noise(key, dims, deviation, reach, pieces=(), kind=jnp.bfloat16):
    drawn = deviation * jax.random.normal(key, dims, jnp.float32)
    if pieces:
        drawn = drawn * levels(key, dims, pieces, -0.22, 0.18)
    return jnp.clip(drawn, -reach, reach).astype(kind)


def gaussian_with(own_key, shape, scale, most, cuts, heavy, kind=jnp.bfloat16):
    values = scale * jax.random.normal(own_key, shape, jnp.float32)
    if cuts:
        values = values * levels(own_key, shape, cuts, -0.22, 0.18)
    return jnp.clip(spiked(values, jax.random.fold_in(own_key, 3), *heavy), -most, most).astype(kind)


def setup_inputs(seed: int = 0) -> dict:
    streams_of = jax.random.split(jax.random.key(seed), 6)
    return {
        "query_hidden": gaussian_with(streams_of[0], (NQ, D), 1.0, 6.0, ((0, 32),), (0, 1, 32, 2.75)),
        "passage_hidden": gaussian_with(streams_of[1], (NQ, D), 1.0, 6.0, ((0, 32),), (0, 1, 32, 2.75)),
        "head_weight": noise(streams_of[2], (D, D), D ** -0.5, 0.09375, ((1, 4),)),
        "neg_blocks": draw_neg_blocks(jax.random.fold_in(streams_of[5], 71), 0),
        "pos_ids": place_ends(jax.random.randint(streams_of[4], (NQ,), 0, BLK), jax.random.fold_in(streams_of[4], 1), 0, BLK - 1).astype(jnp.int32),
    }


logit_divisor = 0.02
epsilon = 1e-06

def normalize(embedding):
    inverse = lax.rsqrt(lax.optimization_barrier(jnp.sum(embedding * embedding, axis=1)) + epsilon)
    return (inverse, embedding * inverse[:, None])

def back_norm(inverse, unit_rows, d_unit):
    inner = lax.optimization_barrier(jnp.sum(unit_rows * d_unit, axis=1))
    return (inverse[:, None] * (d_unit - unit_rows * inner[:, None])).astype(jnp.bfloat16)

def input_gradient(d_embed, head_weight):
    group_width = D // N_MP
    summed = jnp.zeros((d_embed.shape[0], D), jnp.float32)
    for group in range(N_MP):
        lower = group * group_width
        grad_slice = d_embed[:, lower:lower + group_width]
        weight_slice = head_weight[:, lower:lower + group_width]
        partial_sum = jnp.dot(grad_slice, weight_slice.T, preferred_element_type=jnp.float32)
        rounded = lax.optimization_barrier(partial_sum.astype(jnp.bfloat16))
        summed = summed + rounded.astype(jnp.float32)
    return summed.astype(jnp.bfloat16)

def reference(query_hidden, passage_hidden, head_weight, neg_blocks, pos_ids):
    query_embed = jnp.dot(query_hidden, head_weight, preferred_element_type=jnp.float32)
    passage_embed = jnp.dot(passage_hidden, head_weight, preferred_element_type=jnp.float32)
    query_inv, query_unit = normalize(query_embed)
    passage_inv, passage_unit = normalize(passage_embed)
    query_norm = query_unit.astype(jnp.bfloat16)
    passage_norm = passage_unit.astype(jnp.bfloat16)
    query_blocks = query_norm.reshape(NQB, BLK, D)
    passage_blocks = passage_norm.reshape(NQB, BLK, D)
    block_lists = jnp.concatenate([jnp.arange(NQB, dtype=jnp.int32)[:, None], neg_blocks.astype(jnp.int32)], axis=1)
    positions = pos_ids.astype(jnp.int32).reshape(NQB, BLK)
    columns = jnp.arange((1 + K) * BLK, dtype=jnp.int32)

    def visit(d_passage, inputs):
        request_vectors, chosen, target = inputs
        retrieved_documents = jnp.take(passage_blocks, chosen, axis=0).reshape((1 + K) * BLK, D)
        similarity_table = jnp.dot(request_vectors, retrieved_documents.T, preferred_element_type=jnp.float32) / logit_divisor
        matching_document_slot = (columns[None, :] == target[:, None]).astype(jnp.float32)
        exponent_values = jnp.exp(similarity_table)
        normalizer_totals = lax.optimization_barrier(jnp.sum(exponent_values, axis=1))
        losses = jnp.log(normalizer_totals) - lax.optimization_barrier(jnp.sum(similarity_table * matching_document_slot, axis=1))
        attention_probabilities = ((exponent_values / normalizer_totals[:, None] - matching_document_slot) / logit_divisor).astype(jnp.bfloat16)
        d_query = jnp.dot(attention_probabilities, retrieved_documents, preferred_element_type=jnp.float32)
        d_cand = jnp.dot(attention_probabilities.T, request_vectors, preferred_element_type=jnp.float32).reshape(1 + K, BLK, D)
        rounded = lax.optimization_barrier(d_cand[1:].astype(jnp.bfloat16)).astype(jnp.float32)
        d_passage = d_passage.at[chosen[0]].add(d_cand[0])
        d_passage = d_passage.at[chosen[1:]].add(rounded)
        return (d_passage, (losses, d_query))
    start_grad = jnp.zeros((NQB, BLK, D), jnp.float32)
    d_passage, (losses, d_query) = lax.scan(visit, start_grad, (query_blocks, block_lists, positions))
    query_loss = losses.reshape(NQ)
    d_query_embed = back_norm(query_inv, query_unit, d_query.reshape(NQ, D))
    d_passage_embed = back_norm(passage_inv, passage_unit, d_passage.reshape(NQ, D))
    grad_weight = jnp.dot(query_hidden.T, d_query_embed, preferred_element_type=jnp.float32)
    grad_weight = grad_weight + jnp.dot(passage_hidden.T, d_passage_embed, preferred_element_type=jnp.float32)
    grad_query_hidden = input_gradient(d_query_embed, head_weight)
    grad_passage_hidden = input_gradient(d_passage_embed, head_weight)
    return (query_loss, grad_weight, grad_query_hidden, grad_passage_hidden)
```

```python
import jax
import jax.numpy as jnp
from jax import lax
from jax.sharding import PartitionSpec as P

logit_divisor = 0.02
epsilon = 1e-06


def back_norm(inverse, unit_rows, d_unit, inner):
    return (inverse[:, None] * (d_unit - unit_rows * inner[:, None])).astype(jnp.bfloat16)


def to_pieces(blocks, row_groups, feature_groups):
    count, rows, cols = blocks.shape
    parts = blocks.reshape(
        count, row_groups, rows // row_groups, feature_groups, cols // feature_groups
    )
    return parts.transpose(1, 3, 0, 2, 4).reshape(
        row_groups * feature_groups, count, rows // row_groups, cols // feature_groups
    )


def from_pieces(pieces, row_groups, feature_groups):
    _, count, rows, cols = pieces.shape
    parts = pieces.reshape(row_groups, feature_groups, count, rows, cols)
    return parts.transpose(2, 0, 3, 1, 4).reshape(count, row_groups * rows, feature_groups * cols)


def local(query_hidden, passage_hidden, head_weight, neg_blocks, pos_ids):
    dp_count = lax.axis_size("dp")
    block_count, neg_count = neg_blocks.shape
    row_count = query_hidden.shape[0]
    block_rows = row_count // block_count
    embed_width = head_weight.shape[1]
    cand_rows = (1 + neg_count) * block_rows
    request_count = block_count * neg_count
    total_blocks = dp_count * block_count
    feature_groups = 4
    row_groups = dp_count // feature_groups
    piece_rows = block_rows // row_groups
    piece_cols = embed_width // feature_groups
    all_wanted = lax.all_gather(neg_blocks.reshape(request_count), "dp", tiled=True)
    query_embed = jnp.dot(query_hidden, head_weight, preferred_element_type=jnp.float32)
    passage_embed = jnp.dot(passage_hidden, head_weight, preferred_element_type=jnp.float32)
    query_sq, passage_sq = lax.psum(
        (
            jnp.sum(query_embed * query_embed, axis=1),
            jnp.sum(passage_embed * passage_embed, axis=1),
        ),
        "mp",
    )
    query_inv = lax.rsqrt(query_sq + epsilon)
    passage_inv = lax.rsqrt(passage_sq + epsilon)
    query_unit = query_embed * query_inv[:, None]
    passage_unit = passage_embed * passage_inv[:, None]
    query_norm = query_unit.astype(jnp.bfloat16)
    passage_norm = passage_unit.astype(jnp.bfloat16)
    query_blocks = query_norm.reshape(block_count, block_rows, embed_width)
    passage_blocks = passage_norm.reshape(block_count, block_rows, embed_width)
    pieces = to_pieces(passage_blocks, row_groups, feature_groups)
    held = lax.all_to_all(pieces, "dp", split_axis=0, concat_axis=0, tiled=True)
    held = held.reshape(total_blocks, piece_rows, piece_cols)
    reply = jnp.take(held, all_wanted, axis=0).reshape(
        dp_count, request_count, piece_rows, piece_cols
    )
    arrived = lax.all_to_all(reply, "dp", split_axis=0, concat_axis=0, tiled=True)
    fetched = from_pieces(arrived, row_groups, feature_groups).reshape(
        block_count, neg_count, block_rows, embed_width
    )
    retrieved_documents = jnp.concatenate([passage_blocks[:, None], fetched], axis=1).reshape(
        block_count, cand_rows, embed_width
    )
    similarity_parts = jnp.einsum(
        "bqe,bce->bqc", query_blocks, retrieved_documents, preferred_element_type=jnp.float32
    )
    positions = pos_ids.reshape(block_count, block_rows)
    similarity_table = (
        lax.psum(similarity_parts.astype(jnp.bfloat16), "mp").astype(jnp.float32) / logit_divisor
    )
    columns = jnp.arange(cand_rows, dtype=jnp.int32)
    matching_document_slot = (columns[None, None, :] == positions[:, :, None]).astype(jnp.float32)
    exponent_values = jnp.exp(similarity_table)
    normalizer_totals = jnp.sum(exponent_values, axis=2)
    losses = jnp.log(normalizer_totals) - jnp.sum(similarity_table * matching_document_slot, axis=2)
    attention_probabilities = (
        (exponent_values / normalizer_totals[:, :, None] - matching_document_slot) / logit_divisor
    ).astype(jnp.bfloat16)
    d_query = jnp.einsum(
        "bqc,bce->bqe",
        attention_probabilities,
        retrieved_documents,
        preferred_element_type=jnp.float32,
    ).reshape(row_count, embed_width)
    d_cand = jnp.einsum(
        "bqc,bqe->bce", attention_probabilities, query_blocks, preferred_element_type=jnp.float32
    )
    own_terms = d_cand[:, :block_rows]
    neg_terms = (
        d_cand[:, block_rows:].reshape(request_count, block_rows, embed_width).astype(jnp.bfloat16)
    )
    outgoing = to_pieces(neg_terms, row_groups, feature_groups)
    returned = lax.all_to_all(outgoing, "dp", split_axis=0, concat_axis=0, tiled=True)
    selector = (
        all_wanted[None, :] == jnp.arange(total_blocks, dtype=jnp.int32)[:, None]
    ).astype(jnp.bfloat16)
    summed = jnp.dot(
        selector,
        returned.reshape(dp_count * request_count, piece_rows * piece_cols),
        preferred_element_type=jnp.float32,
    ).astype(jnp.bfloat16)
    summed = summed.reshape(dp_count, block_count, piece_rows, piece_cols)
    home = lax.all_to_all(summed, "dp", split_axis=0, concat_axis=0, tiled=True)
    d_passage = own_terms + from_pieces(home, row_groups, feature_groups).astype(jnp.float32)
    d_passage = d_passage.reshape(row_count, embed_width)
    query_inner, passage_inner = lax.psum(
        (jnp.sum(query_unit * d_query, axis=1), jnp.sum(passage_unit * d_passage, axis=1)), "mp"
    )
    d_query_embed = back_norm(query_inv, query_unit, d_query, query_inner)
    d_passage_embed = back_norm(passage_inv, passage_unit, d_passage, passage_inner)
    contract = (((0,), (0,)), ((), ()))
    query_part = lax.dot_general(
        query_hidden, d_query_embed, contract, preferred_element_type=jnp.float32
    )
    passage_part = lax.dot_general(
        passage_hidden, d_passage_embed, contract, preferred_element_type=jnp.float32
    )
    grad_weight = lax.psum_scatter(
        (query_part + passage_part).astype(jnp.bfloat16), "dp", scatter_dimension=0, tiled=True
    ).astype(jnp.float32)
    transpose_dims = (((1,), (1,)), ((), ()))
    query_back = lax.dot_general(
        d_query_embed, head_weight, transpose_dims, preferred_element_type=jnp.float32
    ).astype(jnp.bfloat16)
    passage_back = lax.dot_general(
        d_passage_embed, head_weight, transpose_dims, preferred_element_type=jnp.float32
    ).astype(jnp.bfloat16)
    query_grad, passage_grad = (
        lax.psum_scatter(query_back, "mp", scatter_dimension=1, tiled=True).astype(jnp.float32),
        lax.psum_scatter(passage_back, "mp", scatter_dimension=1, tiled=True).astype(jnp.float32),
    )
    return (
        losses.reshape(row_count),
        grad_weight,
        query_grad.astype(jnp.bfloat16),
        passage_grad.astype(jnp.bfloat16),
    )


def solution(mesh):
    placed = (P("dp", None), P("dp", None), P(None, "mp"), P("dp", None), P("dp"))
    return jax.shard_map(
        local,
        mesh=mesh,
        in_specs=placed,
        out_specs=(P("dp"), P("dp", "mp"), P("dp", "mp"), P("dp", "mp")),
        check_vma=False,
    )
```

```python
import jax
import jax.numpy as jnp
from jax import lax
from jax.experimental import pallas as pl
from jax.experimental.pallas import tpu as pltpu
from jax.sharding import PartitionSpec as P

logit_divisor = 0.02
epsilon = 1e-06


def back_norm(inverse, unit_rows, d_unit, inner):
    return (inverse[:, None] * (d_unit - unit_rows * inner[:, None])).astype(jnp.bfloat16)


MESH = pl.DeviceIdType.MESH
ROW_CONTRACT = (((0,), (0,)), ((), ()))
COL_CONTRACT = (((1,), (1,)), ((), ()))
VMEM_LIMIT = 66 * 1024 * 1024 - 4 * 1024 * 1024


def greet(partners):
    barrier = pltpu.get_barrier_semaphore()
    for partner in partners:
        pl.semaphore_signal(barrier, 1, device_id=partner, device_id_type=MESH)
    pl.semaphore_wait(barrier, len(partners))


def remote(src, dst, send_sem, recv_sem, partner):
    return pltpu.make_async_remote_copy(
        src_ref=src,
        dst_ref=dst,
        send_sem=send_sem,
        recv_sem=recv_sem,
        device_id=partner,
        device_id_type=MESH,
    )


def depth_partner(k):
    return {"mp": lax.rem(lax.axis_index("mp") + k, 4)}


def head_load(head_hbm, head, load_sem, k):
    width = head.shape[1]
    owner = lax.rem(lax.axis_index("mp") + k, 4)
    return pltpu.make_async_copy(
        head_hbm.at[pl.ds(pl.multiple_of(owner * width, width), width)], head.at[k], load_sem.at[k]
    )


def hidden_send(part, landed, send_sem, recv_sem, k):
    return remote(
        part.at[k], landed.at[k - 1], send_sem.at[k - 1], recv_sem.at[k - 1], depth_partner(k)
    )


DEPTH_ORDER = (2, 1, 3, 0)


def hidden_parts(grad, head_hbm, head, part, landed, load_sem, send_sem, recv_sem):
    for k in DEPTH_ORDER:
        head_load(head_hbm, head, load_sem, k).wait()
        half = grad.shape[0] // 2

        @pl.loop(0, 2)
        def _(i):
            rows = pl.ds(pl.multiple_of(i * half, half), half)
            part[k, rows] = lax.dot_general(
                grad[rows], head[k], COL_CONTRACT, preferred_element_type=jnp.float32
            ).astype(jnp.bfloat16)

        if k:
            hidden_send(part, landed, send_sem, recv_sem, k).start()


def hidden_sum(part, landed, send_sem, recv_sem, out):
    for k in (1, 3, 2):
        hidden_send(part, landed, send_sem, recv_sem, k).wait_recv()
    rows_step = 64

    @pl.loop(0, out.shape[0] // rows_step)
    def _(i):
        rows = pl.ds(pl.multiple_of(i * rows_step, rows_step), rows_step)
        total = part[0, rows].astype(jnp.float32)
        for k in range(3):
            total = total + landed[k, rows].astype(jnp.float32)
        out[rows] = total.astype(jnp.bfloat16)

    for k in (1, 3, 2):
        hidden_send(part, landed, send_sem, recv_sem, k).wait_send()


def hidden_kernel(grad, head_hbm, out, head, part, landed, load_sem, send_sem, recv_sem):
    for k in DEPTH_ORDER:
        head_load(head_hbm, head, load_sem, k).start()
    greet([depth_partner(k) for k in (1, 2, 3)])
    hidden_parts(grad, head_hbm, head, part, landed, load_sem, send_sem, recv_sem)
    hidden_sum(part, landed, send_sem, recv_sem, out)


def hidden_grad(grad, head_weight):
    rows, width = grad.shape
    return pl.pallas_call(
        hidden_kernel,
        out_shape=jax.ShapeDtypeStruct((rows, width), jnp.bfloat16),
        in_specs=[pl.BlockSpec(memory_space=pltpu.VMEM), pl.BlockSpec(memory_space=pl.ANY)],
        out_specs=pl.BlockSpec(memory_space=pltpu.VMEM),
        scratch_shapes=[
            pltpu.VMEM((4, width, width), jnp.bfloat16),
            pltpu.VMEM((4, rows, width), jnp.bfloat16),
            pltpu.VMEM((3, rows, width), jnp.bfloat16),
            pltpu.SemaphoreType.DMA((4,)),
            pltpu.SemaphoreType.DMA((3,)),
            pltpu.SemaphoreType.DMA((3,)),
        ],
        compiler_params=pltpu.CompilerParams(
            collective_id=1, has_side_effects=True, vmem_limit_bytes=32 * 1024 * 1024
        ),
        name="hidden_grad",
    )(grad, head_weight)


def place():
    dp = lax.axis_index("dp")
    return lax.div(dp, 8), lax.rem(lax.div(dp, 2), 4), lax.rem(dp, 2)


def at(y, x, core):
    return {"dp": y * 8 + x * 2 + core}


def tail_kernel(
    d_query,
    d_passage,
    query_hbm,
    passage_hbm,
    head_hbm,
    weight_out,
    hidden_out,
    head,
    query,
    passage,
    summed,
    sibling_in,
    pair,
    first_in,
    second_out,
    second_in,
    part,
    landed,
    load_sem,
    hidden_load_sem,
    depth_send,
    depth_recv,
    core_send,
    core_recv,
    first_send,
    first_recv,
    second_send,
    second_recv,
):
    y, x, core = place()
    wide = query.shape[1]
    rows = weight_out.shape[0]
    half = weight_out.shape[1] // 2

    def chunk_of(i):
        return lax.rem(y + 1 + lax.div(i, 2), 4) * 2 + lax.rem(lax.div(x, 2) + 1 + i, 2)

    def hidden_loads(i, slot):
        columns = pl.ds(pl.multiple_of(chunk_of(i) * wide, wide), wide)
        return (
            pltpu.make_async_copy(
                query_hbm.at[:, columns], query.at[slot], hidden_load_sem.at[0, slot]
            ),
            pltpu.make_async_copy(
                passage_hbm.at[:, columns], passage.at[slot], hidden_load_sem.at[1, slot]
            ),
        )

    for k in DEPTH_ORDER:
        head_load(head_hbm, head, load_sem, k).start()
    for copy in hidden_loads(0, 0) + hidden_loads(1, 1):
        copy.start()
    greet(
        [depth_partner(k) for k in (1, 2, 3)]
        + [at(y, x, 1 - core)]
        + [at(lax.rem(y + k, 4), x, core) for k in (1, 2, 3)]
        + [at(y, lax.rem(x + k, 4), core) for k in (1, 2, 3)]
    )
    hidden_parts(d_passage, head_hbm, head, part, landed, load_sem, depth_send, depth_recv)

    def core_copy(chip):
        return remote(
            summed.at[chip, 1 - core],
            sibling_in.at[chip],
            core_send.at[chip],
            core_recv.at[chip],
            at(y, x, 1 - core),
        )

    def first_x(chip):
        to_y, to_x = lax.div(chip, 4), lax.rem(chip, 4)
        k = lax.rem(to_x - x + 4, 4)
        slot = lax.rem(k + 3, 4)
        return k, remote(
            pair.at[chip, 0],
            first_in.at[0, slot, to_y],
            first_send.at[0, chip],
            first_recv.at[0, slot, to_y],
            at(y, to_x, core),
        )

    def first_y(chip):
        to_y, to_x = lax.div(chip, 4), lax.rem(chip, 4)
        k = lax.rem(to_y - y + 4, 4)
        slot = lax.rem(k + 3, 4)
        return k, remote(
            pair.at[chip, 1],
            first_in.at[1, slot, to_x],
            first_send.at[1, chip],
            first_recv.at[1, slot, to_x],
            at(to_y, x, core),
        )

    def produce(i):
        slot = lax.rem(i, 2)
        for copy in hidden_loads(i, slot):
            copy.wait()
        chunk = chunk_of(i)
        for j in range(2):
            columns = slice(j * 2 * rows, (j + 1) * 2 * rows)
            total = lax.dot_general(
                query[slot, :, columns], d_query[...], ROW_CONTRACT, preferred_element_type=jnp.float32
            ) + lax.dot_general(
                passage[slot, :, columns],
                d_passage[...],
                ROW_CONTRACT,
                preferred_element_type=jnp.float32,
            )
            summed[chunk * 2 + j] = total.astype(jnp.bfloat16).reshape(2, rows, 2 * half)
            core_copy(chunk * 2 + j).start()

        @pl.when(i < 6)
        def _():
            for copy in hidden_loads(i + 2, slot):
                copy.start()

    def combine(i):
        for j in range(2):
            chip = chunk_of(i) * 2 + j
            core_copy(chip).wait_recv()
            total = (
                summed[chip, core].astype(jnp.float32) + sibling_in[chip].astype(jnp.float32)
            ).astype(jnp.bfloat16)
            pair[chip, 0] = total[:, :half]
            pair[chip, 1] = total[:, half:]
            for first in (first_x, first_y):
                k, copy = first(chip)

                @pl.when(k != 0)
                def _():
                    copy.start()

    @pl.loop(0, 9)
    def _(i):
        @pl.when(i < 8)
        def _():
            produce(i)

        @pl.when(i > 0)
        def _():
            combine(i - 1)

    def first_arrival(side, k, other):
        return remote(
            first_in.at[side, k, other],
            first_in.at[side, k, other],
            first_send.at[side, 0],
            first_recv.at[side, k, other],
            at(y, x, 1 - core),
        )

    def gathered(side, other):
        chip = other * 4 + x if side == 0 else y * 4 + other
        total = pair[chip, side].astype(jnp.float32)
        for k in range(3):
            first_arrival(side, k, other).wait_recv()
            total = total + first_in[side, k, other].astype(jnp.float32)
        return total

    def second_copy(side, k):
        if side == 0:
            partner = at(lax.rem(y + k, 4), x, core)
        else:
            partner = at(y, lax.rem(x + k, 4), core)
        return remote(
            second_out.at[side, k - 1],
            second_in.at[side, k - 1],
            second_send.at[side, k - 1],
            second_recv.at[side, k - 1],
            partner,
        )

    for k in (1, 2, 3):
        for side in range(2):
            base = y if side == 0 else x
            second_out[side, k - 1] = gathered(side, lax.rem(base + k, 4)).astype(jnp.bfloat16)
            second_copy(side, k).start()
    for side in range(2):
        weight_out[:, side * half : (side + 1) * half] = gathered(side, y if side == 0 else x)
    for side in range(2):
        for k in (1, 2, 3):
            second_copy(side, k).wait_recv()
            weight_out[:, side * half : (side + 1) * half] += second_in[side, k - 1].astype(
                jnp.float32
            )
    hidden_sum(part, landed, depth_send, depth_recv, hidden_out)

    @pl.loop(0, 16)
    def _(chip):
        core_copy(chip).wait_send()
        for first in (first_x, first_y):
            k, copy = first(chip)

            @pl.when(k != 0)
            def _():
                copy.wait_send()

    for side in range(2):
        for k in (1, 2, 3):
            second_copy(side, k).wait_send()


def tail(d_query, d_passage, query_hidden, passage_hidden, head_weight):
    rows, width = d_query.shape
    hidden = head_weight.shape[0]
    share = hidden // 32
    bf16 = jnp.bfloat16
    vmem = pl.BlockSpec(memory_space=pltpu.VMEM)
    hbm = pl.BlockSpec(memory_space=pl.ANY)
    dma = pltpu.SemaphoreType.DMA
    return pl.pallas_call(
        tail_kernel,
        out_shape=(
            jax.ShapeDtypeStruct((share, width), jnp.float32),
            jax.ShapeDtypeStruct((rows, width), bf16),
        ),
        in_specs=[vmem, vmem, hbm, hbm, hbm],
        out_specs=(vmem, vmem),
        scratch_shapes=[
            pltpu.VMEM((4, width, width), bf16),
            pltpu.VMEM((2, rows, 4 * share), bf16),
            pltpu.VMEM((2, rows, 4 * share), bf16),
            pltpu.VMEM((16, 2, share, width), bf16),
            pltpu.VMEM((16, share, width), bf16),
            pltpu.VMEM((16, 2, share, width // 2), bf16),
            pltpu.VMEM((2, 3, 4, share, width // 2), bf16),
            pltpu.VMEM((2, 3, share, width // 2), bf16),
            pltpu.VMEM((2, 3, share, width // 2), bf16),
            pltpu.VMEM((4, rows, width), bf16),
            pltpu.VMEM((3, rows, width), bf16),
            dma((4,)),
            dma((2, 2)),
            dma((3,)),
            dma((3,)),
            dma((16,)),
            dma((16,)),
            dma((2, 16)),
            dma((2, 3, 4)),
            dma((2, 3)),
            dma((2, 3)),
        ],
        compiler_params=pltpu.CompilerParams(
            collective_id=2, has_side_effects=True, vmem_limit_bytes=VMEM_LIMIT
        ),
        name="tail",
    )(d_query, d_passage, query_hidden, passage_hidden, head_weight)


def to_pieces(blocks, row_groups, feature_groups):
    count, rows, cols = blocks.shape
    parts = blocks.reshape(
        count, row_groups, rows // row_groups, feature_groups, cols // feature_groups
    )
    return parts.transpose(1, 3, 0, 2, 4).reshape(
        row_groups * feature_groups, count, rows // row_groups, cols // feature_groups
    )


def from_pieces(pieces, row_groups, feature_groups):
    _, count, rows, cols = pieces.shape
    parts = pieces.reshape(row_groups, feature_groups, count, rows, cols)
    return parts.transpose(2, 0, 3, 1, 4).reshape(count, row_groups * rows, feature_groups * cols)


def local(query_hidden, passage_hidden, head_weight, neg_blocks, pos_ids):
    dp_count = lax.axis_size("dp")
    block_count, neg_count = neg_blocks.shape
    row_count = query_hidden.shape[0]
    block_rows = row_count // block_count
    embed_width = head_weight.shape[1]
    cand_rows = (1 + neg_count) * block_rows
    request_count = block_count * neg_count
    total_blocks = dp_count * block_count
    feature_groups = 4
    row_groups = dp_count // feature_groups
    piece_rows = block_rows // row_groups
    piece_cols = embed_width // feature_groups
    all_wanted = lax.all_gather(neg_blocks.reshape(request_count), "dp", tiled=True)
    query_embed = jnp.dot(query_hidden, head_weight, preferred_element_type=jnp.float32)
    passage_embed = jnp.dot(passage_hidden, head_weight, preferred_element_type=jnp.float32)
    query_sq, passage_sq = lax.psum(
        (
            jnp.sum(query_embed * query_embed, axis=1),
            jnp.sum(passage_embed * passage_embed, axis=1),
        ),
        "mp",
    )
    query_inv = lax.rsqrt(query_sq + epsilon)
    passage_inv = lax.rsqrt(passage_sq + epsilon)
    query_unit = query_embed * query_inv[:, None]
    passage_unit = passage_embed * passage_inv[:, None]
    query_norm = query_unit.astype(jnp.bfloat16)
    passage_norm = passage_unit.astype(jnp.bfloat16)
    query_blocks = query_norm.reshape(block_count, block_rows, embed_width)
    passage_blocks = passage_norm.reshape(block_count, block_rows, embed_width)
    pieces = to_pieces(passage_blocks, row_groups, feature_groups)
    held = lax.all_to_all(pieces, "dp", split_axis=0, concat_axis=0, tiled=True)
    held = held.reshape(total_blocks, piece_rows, piece_cols)
    reply = jnp.take(held, all_wanted, axis=0).reshape(
        dp_count, request_count, piece_rows, piece_cols
    )
    arrived = lax.all_to_all(reply, "dp", split_axis=0, concat_axis=0, tiled=True)
    fetched = from_pieces(arrived, row_groups, feature_groups).reshape(
        block_count, neg_count, block_rows, embed_width
    )
    retrieved_documents = jnp.concatenate([passage_blocks[:, None], fetched], axis=1).reshape(
        block_count, cand_rows, embed_width
    )
    similarity_parts = jnp.einsum(
        "bqe,bce->bqc", query_blocks, retrieved_documents, preferred_element_type=jnp.float32
    )
    positions = pos_ids.reshape(block_count, block_rows)
    similarity_table = (
        lax.psum(similarity_parts.astype(jnp.bfloat16), "mp").astype(jnp.float32) / logit_divisor
    )
    columns = jnp.arange(cand_rows, dtype=jnp.int32)
    matching_document_slot = (columns[None, None, :] == positions[:, :, None]).astype(jnp.float32)
    exponent_values = jnp.exp(similarity_table)
    normalizer_totals = jnp.sum(exponent_values, axis=2)
    losses = jnp.log(normalizer_totals) - jnp.sum(similarity_table * matching_document_slot, axis=2)
    attention_probabilities = (
        (exponent_values / normalizer_totals[:, :, None] - matching_document_slot) / logit_divisor
    ).astype(jnp.bfloat16)
    d_query = jnp.einsum(
        "bqc,bce->bqe",
        attention_probabilities,
        retrieved_documents,
        preferred_element_type=jnp.float32,
    ).reshape(row_count, embed_width)
    d_cand = jnp.einsum(
        "bqc,bqe->bce", attention_probabilities, query_blocks, preferred_element_type=jnp.float32
    )
    own_terms = d_cand[:, :block_rows]
    neg_terms = (
        d_cand[:, block_rows:].reshape(request_count, block_rows, embed_width).astype(jnp.bfloat16)
    )
    outgoing = to_pieces(neg_terms, row_groups, feature_groups)
    returned = lax.all_to_all(outgoing, "dp", split_axis=0, concat_axis=0, tiled=True)
    selector = (
        all_wanted[None, :] == jnp.arange(total_blocks, dtype=jnp.int32)[:, None]
    ).astype(jnp.bfloat16)
    summed = jnp.dot(
        selector,
        returned.reshape(dp_count * request_count, piece_rows * piece_cols),
        preferred_element_type=jnp.float32,
    ).astype(jnp.bfloat16)
    summed = summed.reshape(dp_count, block_count, piece_rows, piece_cols)
    home = lax.all_to_all(summed, "dp", split_axis=0, concat_axis=0, tiled=True)
    d_passage = own_terms + from_pieces(home, row_groups, feature_groups).astype(jnp.float32)
    d_passage = d_passage.reshape(row_count, embed_width)
    query_inner = lax.psum(jnp.sum(query_unit * d_query, axis=1), "mp")
    passage_inner = lax.psum(jnp.sum(passage_unit * d_passage, axis=1), "mp")
    d_query_embed = back_norm(query_inv, query_unit, d_query, query_inner)
    d_passage_embed = back_norm(passage_inv, passage_unit, d_passage, passage_inner)
    query_grad = hidden_grad(d_query_embed, head_weight)
    grad_weight, passage_grad = tail(
        d_query_embed, d_passage_embed, query_hidden, passage_hidden, head_weight
    )
    return (
        losses.reshape(row_count),
        grad_weight,
        query_grad,
        passage_grad,
    )


def solution(mesh):
    placed = (P("dp", None), P("dp", None), P(None, "mp"), P("dp", None), P("dp"))
    return jax.shard_map(
        local,
        mesh=mesh,
        in_specs=placed,
        out_specs=(P("dp"), P("dp", "mp"), P("dp", "mp"), P("dp", "mp")),
        check_vma=False,
    )
```

```python
import jax
import jax.numpy as jnp
from jax import lax
from jax.experimental import pallas as pl
from jax.experimental.pallas import tpu as pltpu
from jax.sharding import PartitionSpec as P

logit_divisor = 0.02
epsilon = 1e-06


def back_norm(inverse, unit_rows, d_unit, inner):
    return (inverse[:, None] * (d_unit - unit_rows * inner[:, None])).astype(jnp.bfloat16)


MESH = pl.DeviceIdType.MESH
ROW_CONTRACT = (((0,), (0,)), ((), ()))
COL_CONTRACT = (((1,), (1,)), ((), ()))
VMEM_LIMIT = 66 * 1024 * 1024 - 4 * 1024 * 1024


def greet(partners):
    barrier = pltpu.get_barrier_semaphore()
    for partner in partners:
        pl.semaphore_signal(barrier, 1, device_id=partner, device_id_type=MESH)
    pl.semaphore_wait(barrier, len(partners))


def remote(src, dst, send_sem, recv_sem, partner):
    return pltpu.make_async_remote_copy(
        src_ref=src,
        dst_ref=dst,
        send_sem=send_sem,
        recv_sem=recv_sem,
        device_id=partner,
        device_id_type=MESH,
    )


def depth_partner(k):
    return {"mp": lax.rem(lax.axis_index("mp") + k, 4)}


def head_load(head_hbm, head, load_sem, k):
    width = head.shape[1]
    owner = lax.rem(lax.axis_index("mp") + k, 4)
    return pltpu.make_async_copy(
        head_hbm.at[pl.ds(pl.multiple_of(owner * width, width), width)], head.at[k], load_sem.at[k]
    )


def hidden_send(part, landed, send_sem, recv_sem, k):
    return remote(
        part.at[k], landed.at[k - 1], send_sem.at[k - 1], recv_sem.at[k - 1], depth_partner(k)
    )


DEPTH_ORDER = (2, 1, 3, 0)


def hidden_parts(grad, head_hbm, head, part, landed, load_sem, send_sem, recv_sem):
    for k in DEPTH_ORDER:
        head_load(head_hbm, head, load_sem, k).wait()
        half = grad.shape[0] // 2

        @pl.loop(0, 2)
        def _(i):
            rows = pl.ds(pl.multiple_of(i * half, half), half)
            part[k, rows] = lax.dot_general(
                grad[rows], head[k], COL_CONTRACT, preferred_element_type=jnp.float32
            ).astype(jnp.bfloat16)

        if k:
            hidden_send(part, landed, send_sem, recv_sem, k).start()


def hidden_sum(part, landed, send_sem, recv_sem, out):
    for k in (1, 3, 2):
        hidden_send(part, landed, send_sem, recv_sem, k).wait_recv()
    rows_step = 64

    @pl.loop(0, out.shape[0] // rows_step)
    def _(i):
        rows = pl.ds(pl.multiple_of(i * rows_step, rows_step), rows_step)
        total = part[0, rows].astype(jnp.float32)
        for k in range(3):
            total = total + landed[k, rows].astype(jnp.float32)
        out[rows] = total.astype(jnp.bfloat16)

    for k in (1, 3, 2):
        hidden_send(part, landed, send_sem, recv_sem, k).wait_send()


def hidden_kernel(grad, head_hbm, out, head, part, landed, load_sem, send_sem, recv_sem):
    for k in DEPTH_ORDER:
        head_load(head_hbm, head, load_sem, k).start()
    greet([depth_partner(k) for k in (1, 2, 3)])
    hidden_parts(grad, head_hbm, head, part, landed, load_sem, send_sem, recv_sem)
    hidden_sum(part, landed, send_sem, recv_sem, out)


def hidden_grad(grad, head_weight):
    rows, width = grad.shape
    return pl.pallas_call(
        hidden_kernel,
        out_shape=jax.ShapeDtypeStruct((rows, width), jnp.bfloat16),
        in_specs=[pl.BlockSpec(memory_space=pltpu.VMEM), pl.BlockSpec(memory_space=pl.ANY)],
        out_specs=pl.BlockSpec(memory_space=pltpu.VMEM),
        scratch_shapes=[
            pltpu.VMEM((4, width, width), jnp.bfloat16),
            pltpu.VMEM((4, rows, width), jnp.bfloat16),
            pltpu.VMEM((3, rows, width), jnp.bfloat16),
            pltpu.SemaphoreType.DMA((4,)),
            pltpu.SemaphoreType.DMA((3,)),
            pltpu.SemaphoreType.DMA((3,)),
        ],
        compiler_params=pltpu.CompilerParams(
            collective_id=1, has_side_effects=True, vmem_limit_bytes=32 * 1024 * 1024
        ),
        name="hidden_grad",
    )(grad, head_weight)


def place():
    dp = lax.axis_index("dp")
    return lax.div(dp, 8), lax.rem(lax.div(dp, 2), 4), lax.rem(dp, 2)


def at(y, x, core):
    return {"dp": y * 8 + x * 2 + core}


def tail_kernel(
    d_query,
    d_passage,
    query_hbm,
    passage_hbm,
    head_hbm,
    weight_out,
    hidden_out,
    head,
    query,
    passage,
    summed,
    sibling_in,
    pair,
    first_in,
    second_out,
    second_in,
    part,
    landed,
    load_sem,
    hidden_load_sem,
    depth_send,
    depth_recv,
    core_send,
    core_recv,
    first_send,
    first_recv,
    second_send,
    second_recv,
):
    y, x, core = place()
    wide = query.shape[1]
    rows = weight_out.shape[0]
    half = weight_out.shape[1] // 2

    def chunk_of(i):
        return lax.rem(y + 1 + lax.div(i, 2), 4) * 2 + lax.rem(lax.div(x, 2) + 1 + i, 2)

    def hidden_loads(i, slot):
        columns = pl.ds(pl.multiple_of(chunk_of(i) * wide, wide), wide)
        return (
            pltpu.make_async_copy(
                query_hbm.at[:, columns], query.at[slot], hidden_load_sem.at[0, slot]
            ),
            pltpu.make_async_copy(
                passage_hbm.at[:, columns], passage.at[slot], hidden_load_sem.at[1, slot]
            ),
        )

    for k in DEPTH_ORDER:
        head_load(head_hbm, head, load_sem, k).start()
    for copy in hidden_loads(0, 0) + hidden_loads(1, 1):
        copy.start()
    greet(
        [depth_partner(k) for k in (1, 2, 3)]
        + [at(y, x, 1 - core)]
        + [at(lax.rem(y + k, 4), x, core) for k in (1, 2, 3)]
        + [at(y, lax.rem(x + k, 4), core) for k in (1, 2, 3)]
    )
    hidden_parts(d_passage, head_hbm, head, part, landed, load_sem, depth_send, depth_recv)

    def core_copy(chip):
        return remote(
            summed.at[chip, 1 - core],
            sibling_in.at[chip],
            core_send.at[chip],
            core_recv.at[chip],
            at(y, x, 1 - core),
        )

    def first_x(chip):
        to_y, to_x = lax.div(chip, 4), lax.rem(chip, 4)
        k = lax.rem(to_x - x + 4, 4)
        slot = lax.rem(k + 3, 4)
        return k, remote(
            pair.at[chip, 0],
            first_in.at[0, slot, to_y],
            first_send.at[0, chip],
            first_recv.at[0, slot, to_y],
            at(y, to_x, core),
        )

    def first_y(chip):
        to_y, to_x = lax.div(chip, 4), lax.rem(chip, 4)
        k = lax.rem(to_y - y + 4, 4)
        slot = lax.rem(k + 3, 4)
        return k, remote(
            pair.at[chip, 1],
            first_in.at[1, slot, to_x],
            first_send.at[1, chip],
            first_recv.at[1, slot, to_x],
            at(to_y, x, core),
        )

    def produce(i):
        slot = lax.rem(i, 2)
        for copy in hidden_loads(i, slot):
            copy.wait()
        chunk = chunk_of(i)
        for j in range(2):
            columns = slice(j * 2 * rows, (j + 1) * 2 * rows)
            total = lax.dot_general(
                query[slot, :, columns], d_query[...], ROW_CONTRACT, preferred_element_type=jnp.float32
            ) + lax.dot_general(
                passage[slot, :, columns],
                d_passage[...],
                ROW_CONTRACT,
                preferred_element_type=jnp.float32,
            )
            summed[chunk * 2 + j] = total.astype(jnp.bfloat16).reshape(2, rows, 2 * half)
            core_copy(chunk * 2 + j).start()

        @pl.when(i < 6)
        def _():
            for copy in hidden_loads(i + 2, slot):
                copy.start()

    def combine(i):
        for j in range(2):
            chip = chunk_of(i) * 2 + j
            core_copy(chip).wait_recv()
            total = (
                summed[chip, core].astype(jnp.float32) + sibling_in[chip].astype(jnp.float32)
            ).astype(jnp.bfloat16)
            pair[chip, 0] = total[:, :half]
            pair[chip, 1] = total[:, half:]
            for first in (first_x, first_y):
                k, copy = first(chip)

                @pl.when(k != 0)
                def _():
                    copy.start()

    @pl.loop(0, 9)
    def _(i):
        @pl.when(i < 8)
        def _():
            produce(i)

        @pl.when(i > 0)
        def _():
            combine(i - 1)

    def first_arrival(side, k, other):
        return remote(
            first_in.at[side, k, other],
            first_in.at[side, k, other],
            first_send.at[side, 0],
            first_recv.at[side, k, other],
            at(y, x, 1 - core),
        )

    def gathered(side, other):
        chip = other * 4 + x if side == 0 else y * 4 + other
        total = pair[chip, side].astype(jnp.float32)
        for k in range(3):
            first_arrival(side, k, other).wait_recv()
            total = total + first_in[side, k, other].astype(jnp.float32)
        return total

    def second_copy(side, k):
        if side == 0:
            partner = at(lax.rem(y + k, 4), x, core)
        else:
            partner = at(y, lax.rem(x + k, 4), core)
        return remote(
            second_out.at[side, k - 1],
            second_in.at[side, k - 1],
            second_send.at[side, k - 1],
            second_recv.at[side, k - 1],
            partner,
        )

    for k in (1, 2, 3):
        for side in range(2):
            base = y if side == 0 else x
            second_out[side, k - 1] = gathered(side, lax.rem(base + k, 4)).astype(jnp.bfloat16)
            second_copy(side, k).start()
    for side in range(2):
        weight_out[:, side * half : (side + 1) * half] = gathered(side, y if side == 0 else x)
    for side in range(2):
        for k in (1, 2, 3):
            second_copy(side, k).wait_recv()
            weight_out[:, side * half : (side + 1) * half] += second_in[side, k - 1].astype(
                jnp.float32
            )
    hidden_sum(part, landed, depth_send, depth_recv, hidden_out)

    @pl.loop(0, 16)
    def _(chip):
        core_copy(chip).wait_send()
        for first in (first_x, first_y):
            k, copy = first(chip)

            @pl.when(k != 0)
            def _():
                copy.wait_send()

    for side in range(2):
        for k in (1, 2, 3):
            second_copy(side, k).wait_send()


def tail(d_query, d_passage, query_hidden, passage_hidden, head_weight):
    rows, width = d_query.shape
    hidden = head_weight.shape[0]
    share = hidden // 32
    bf16 = jnp.bfloat16
    vmem = pl.BlockSpec(memory_space=pltpu.VMEM)
    hbm = pl.BlockSpec(memory_space=pl.ANY)
    dma = pltpu.SemaphoreType.DMA
    return pl.pallas_call(
        tail_kernel,
        out_shape=(
            jax.ShapeDtypeStruct((share, width), jnp.float32),
            jax.ShapeDtypeStruct((rows, width), bf16),
        ),
        in_specs=[vmem, vmem, hbm, hbm, hbm],
        out_specs=(vmem, vmem),
        scratch_shapes=[
            pltpu.VMEM((4, width, width), bf16),
            pltpu.VMEM((2, rows, 4 * share), bf16),
            pltpu.VMEM((2, rows, 4 * share), bf16),
            pltpu.VMEM((16, 2, share, width), bf16),
            pltpu.VMEM((16, share, width), bf16),
            pltpu.VMEM((16, 2, share, width // 2), bf16),
            pltpu.VMEM((2, 3, 4, share, width // 2), bf16),
            pltpu.VMEM((2, 3, share, width // 2), bf16),
            pltpu.VMEM((2, 3, share, width // 2), bf16),
            pltpu.VMEM((4, rows, width), bf16),
            pltpu.VMEM((3, rows, width), bf16),
            dma((4,)),
            dma((2, 2)),
            dma((3,)),
            dma((3,)),
            dma((16,)),
            dma((16,)),
            dma((2, 16)),
            dma((2, 3, 4)),
            dma((2, 3)),
            dma((2, 3)),
        ],
        compiler_params=pltpu.CompilerParams(
            collective_id=2, has_side_effects=True, vmem_limit_bytes=VMEM_LIMIT
        ),
        name="tail",
    )(d_query, d_passage, query_hidden, passage_hidden, head_weight)


OFFSETS = tuple(
    (dy, dx, core)
    for dy, dx in (
        (2, 2), (1, 3), (3, 1), (1, 1), (3, 3), (0, 2), (2, 0), (1, 2),
        (3, 2), (2, 1), (2, 3), (0, 1), (1, 0), (0, 3), (3, 0), (0, 0),
    )
    for core in range(2)
    if dy or dx or core
)


def plane_peer(offset):
    y, x, core = place()
    return (
        lax.rem(y + offset[0], 4) * 8 + lax.rem(x + offset[1], 4) * 2 + lax.rem(core + offset[2], 2)
    )


def share_rows(device):
    return pl.ds(pl.multiple_of(lax.div(device, 4) * 16, 16), 16)


def share_cols(device):
    return pl.ds(pl.multiple_of(lax.rem(device, 4) * 256, 256), 256)


def diagonal():
    rows = lax.broadcasted_iota(jnp.int32, (128, 128), 0)
    return rows == lax.broadcasted_iota(jnp.int32, (128, 128), 1)


def as_row(column):
    spread = jnp.broadcast_to(column, (128, 128))
    return jnp.sum(jnp.where(diagonal(), spread, 0.0), axis=0, keepdims=True)


def as_column(row):
    spread = jnp.broadcast_to(row, (128, 128))
    return jnp.sum(jnp.where(diagonal(), spread, 0.0), axis=1, keepdims=True)


def depth_copy(src, dst, send_sem, recv_sem, k):
    return remote(src, dst.at[k - 1], send_sem.at[k - 1], recv_sem.at[k - 1], depth_partner(k))


def depth_start(src, dst, send_sem, recv_sem):
    for k in (2, 1, 3):
        depth_copy(src, dst, send_sem, recv_sem, k).start()


def depth_total(src, dst, send_sem, recv_sem):
    for k in (1, 3, 2):
        depth_copy(src, dst, send_sem, recv_sem, k).wait_recv()
    return src[...] + dst[0] + dst[1] + dst[2]


def depth_finish(src, dst, send_sem, recv_sem):
    for k in (1, 2, 3):
        depth_copy(src, dst, send_sem, recv_sem, k).wait_send()


def front_kernel(
    query_hbm,
    passage_hbm,
    head_hbm,
    wanted,
    positions,
    weights,
    losses,
    query_norm,
    passage_norm,
    inverses,
    fetched,
    all_wanted,
    head,
    hidden,
    embed,
    held,
    reply,
    partial,
    partial_in,
    squares,
    squares_in,
    table,
    load_sem,
    table_sem,
    square_send,
    square_recv,
    want_send,
    want_recv,
    spread_send,
    spread_recv,
    reply_send,
    reply_recv,
    partial_send,
    partial_recv,
    weight_send,
    weight_recv,
    loss_send,
    loss_recv,
):
    dp = lax.axis_index("dp")
    mp = lax.axis_index("mp")
    depth = head.shape[1]
    hidden_hbm = (passage_hbm, query_hbm)

    def hidden_load(side, chunk):
        columns = pl.ds(pl.multiple_of(chunk * depth, depth), depth)
        return pltpu.make_async_copy(
            hidden_hbm[side].at[:, columns], hidden.at[side, chunk], load_sem.at[side, chunk]
        )

    def head_chunk(chunk):
        rows = pl.ds(pl.multiple_of(chunk * depth, depth), depth)
        return pltpu.make_async_copy(head_hbm.at[rows], head.at[chunk], load_sem.at[2, chunk])

    for chunk in range(4):
        hidden_load(0, chunk).start()
        head_chunk(chunk).start()
    for chunk in range(4):
        hidden_load(1, chunk).start()
    embed[...] = jnp.zeros_like(embed)
    greet(
        [{"dp": plane_peer(offset)} for offset in OFFSETS]
        + [depth_partner(k) for k in (1, 2, 3)]
    )

    def want_copy(j):
        return remote(
            wanted,
            all_wanted.at[dp],
            want_send.at[j],
            want_recv.at[j],
            {"dp": plane_peer(OFFSETS[j])},
        )

    for j in range(31):
        want_copy(j).start()
    all_wanted[dp] = wanted[...]

    def project(side):
        @pl.loop(0, 4)
        def _(chunk):
            hidden_load(side, chunk).wait()
            if side == 0:
                head_chunk(chunk).wait()

            @pl.loop(0, 2)
            def _(i):
                rows = pl.ds(pl.multiple_of(i * 256, 256), 256)
                embed[side, rows] += jnp.dot(
                    hidden[side, chunk, rows], head[chunk], preferred_element_type=jnp.float32
                )

        for b in range(4):
            block = embed[side, b * 128 : (b + 1) * 128]
            squares[side, b : b + 1] = as_row(jnp.sum(block * block, axis=1, keepdims=True))
        squares[side, 4:8] = jnp.zeros((4, 128), jnp.float32)

    def square_args(side):
        return squares.at[side], squares_in.at[side], square_send.at[side], square_recv.at[side]

    def normalize(side, out):
        inverses[side] = lax.rsqrt(depth_total(*square_args(side)) + epsilon)
        for b in range(4):
            inverse = as_column(inverses[side, b : b + 1])
            out[b] = (embed[side, b * 128 : (b + 1) * 128] * inverse).astype(jnp.bfloat16)

    project(0)
    depth_start(*square_args(0))
    normalize(0, passage_norm)

    def spread_copy(j):
        peer = plane_peer(OFFSETS[j])
        return remote(
            passage_norm.at[:, share_rows(peer), share_cols(peer)],
            held.at[pl.ds(dp * 4, 4)],
            spread_send.at[j],
            spread_recv.at[j],
            {"dp": peer},
        )

    for j in range(31):
        spread_copy(j).start()
    for b in range(4):
        held[dp * 4 + b] = passage_norm[b, share_rows(dp), share_cols(dp)]
    project(1)
    depth_start(*square_args(1))
    normalize(1, query_norm)
    for j in range(31):
        want_copy(j).wait_recv()
    table_copy = pltpu.make_async_copy(all_wanted, table, table_sem)
    table_copy.start()
    table_copy.wait()
    for j in range(31):
        spread_copy(j).wait_recv()

    def reply_copy(j):
        peer = plane_peer(OFFSETS[j])
        return remote(
            reply.at[peer],
            fetched.at[:, share_rows(dp), share_cols(dp)],
            reply_send.at[j],
            reply_recv.at[j],
            {"dp": peer},
        )

    def gather(device):
        @pl.loop(0, 16, unroll=4)
        def _(i):
            reply[device, i] = held[table[device, i, 0]]

    for j in range(31):
        gather(plane_peer(OFFSETS[j]))
        reply_copy(j).start()
    gather(dp)
    fetched[:, share_rows(dp), share_cols(dp)] = reply[dp]
    for j in range(31):
        reply_copy(j).wait_recv()

    def partial_copy(k):
        return depth_copy(
            partial.at[lax.rem(mp + k, 4)], partial_in, partial_send, partial_recv, k
        )

    for k in DEPTH_ORDER:
        b = lax.rem(mp + k, 4)
        rows = query_norm[b]
        partial[b, :, :128] = lax.dot_general(
            rows, passage_norm[b], COL_CONTRACT, preferred_element_type=jnp.float32
        ).astype(jnp.bfloat16)
        others = fetched[pl.ds(b * 4, 4)].reshape(512, depth)
        partial[b, :, 128:] = lax.dot_general(
            rows, others, COL_CONTRACT, preferred_element_type=jnp.float32
        ).astype(jnp.bfloat16)
        if k:
            partial_copy(k).start()
    scores = partial[mp].astype(jnp.float32)
    for k in (1, 3, 2):
        partial_copy(k).wait_recv()
        scores = scores + partial_in[k - 1].astype(jnp.float32)
    scores = scores / logit_divisor
    columns = lax.broadcasted_iota(jnp.int32, scores.shape, 1).astype(jnp.float32)
    matching = (columns == as_column(positions[pl.ds(mp, 1)])).astype(jnp.float32)
    powers = jnp.exp(scores)
    totals = jnp.sum(powers, axis=1, keepdims=True)
    loss = jnp.log(totals) - jnp.sum(scores * matching, axis=1, keepdims=True)
    weights[mp] = ((powers / totals - matching) / logit_divisor).astype(jnp.bfloat16)
    losses[mp] = jnp.broadcast_to(as_row(loss), (8, 128))

    def weight_copies(k):
        return (
            remote(
                weights.at[mp],
                weights.at[mp],
                weight_send.at[k - 1],
                weight_recv.at[k - 1],
                depth_partner(k),
            ),
            remote(
                losses.at[mp],
                losses.at[mp],
                loss_send.at[k - 1],
                loss_recv.at[k - 1],
                depth_partner(k),
            ),
        )

    for k in (2, 1, 3):
        for copy in weight_copies(k):
            copy.start()
    for j in range(31):
        want_copy(j).wait_send()
        spread_copy(j).wait_send()
        reply_copy(j).wait_send()
    depth_finish(*square_args(0))
    depth_finish(*square_args(1))
    for k in (1, 3, 2):
        partial_copy(k).wait_send()
        for copy in weight_copies(k):
            copy.wait()


def front(query_hidden, passage_hidden, head_weight, neg_blocks, pos_ids):
    bf16 = jnp.bfloat16
    f32 = jnp.float32
    rows = query_hidden.shape[0]
    width = head_weight.shape[1]
    wanted = jnp.broadcast_to(neg_blocks.reshape(16, 1), (16, 128))
    positions = pos_ids.reshape(4, 128).astype(f32)
    vmem = pl.BlockSpec(memory_space=pltpu.VMEM)
    hbm = pl.BlockSpec(memory_space=pl.ANY)
    dma = pltpu.SemaphoreType.DMA
    return pl.pallas_call(
        front_kernel,
        out_shape=(
            jax.ShapeDtypeStruct((4, 128, 640), bf16),
            jax.ShapeDtypeStruct((4, 8, 128), f32),
            jax.ShapeDtypeStruct((4, 128, width), bf16),
            jax.ShapeDtypeStruct((4, 128, width), bf16),
            jax.ShapeDtypeStruct((2, 8, 128), f32),
            jax.ShapeDtypeStruct((16, 128, width), bf16),
            jax.ShapeDtypeStruct((32, 16, 128), jnp.int32),
        ),
        in_specs=[hbm, hbm, hbm, vmem, vmem],
        out_specs=(vmem,) * 7,
        scratch_shapes=[
            pltpu.VMEM((4, width, width), bf16),
            pltpu.VMEM((2, 4, rows, width), bf16),
            pltpu.VMEM((2, rows, width), f32),
            pltpu.VMEM((128, 16, 256), bf16),
            pltpu.VMEM((32, 16, 16, 256), bf16),
            pltpu.VMEM((4, 128, 640), bf16),
            pltpu.VMEM((3, 128, 640), bf16),
            pltpu.VMEM((2, 8, 128), f32),
            pltpu.VMEM((2, 3, 8, 128), f32),
            pltpu.SMEM((32, 16, 128), jnp.int32),
            dma((3, 4)),
            dma,
            dma((2, 3)),
            dma((2, 3)),
            dma((31,)),
            dma((31,)),
            dma((31,)),
            dma((31,)),
            dma((31,)),
            dma((31,)),
            dma((3,)),
            dma((3,)),
            dma((3,)),
            dma((3,)),
            dma((3,)),
            dma((3,)),
        ],
        compiler_params=pltpu.CompilerParams(
            collective_id=3, has_side_effects=True, vmem_limit_bytes=VMEM_LIMIT
        ),
        name="front",
    )(query_hidden, passage_hidden, head_weight, wanted, positions)


def to_pieces(blocks, row_groups, feature_groups):
    count, rows, cols = blocks.shape
    parts = blocks.reshape(
        count, row_groups, rows // row_groups, feature_groups, cols // feature_groups
    )
    return parts.transpose(1, 3, 0, 2, 4).reshape(
        row_groups * feature_groups, count, rows // row_groups, cols // feature_groups
    )


def from_pieces(pieces, row_groups, feature_groups):
    _, count, rows, cols = pieces.shape
    parts = pieces.reshape(row_groups, feature_groups, count, rows, cols)
    return parts.transpose(2, 0, 3, 1, 4).reshape(count, row_groups * rows, feature_groups * cols)


def local(query_hidden, passage_hidden, head_weight, neg_blocks, pos_ids):
    dp_count = lax.axis_size("dp")
    block_count, neg_count = neg_blocks.shape
    row_count = query_hidden.shape[0]
    block_rows = row_count // block_count
    embed_width = head_weight.shape[1]
    cand_rows = (1 + neg_count) * block_rows
    request_count = block_count * neg_count
    total_blocks = dp_count * block_count
    feature_groups = 4
    row_groups = dp_count // feature_groups
    piece_rows = block_rows // row_groups
    piece_cols = embed_width // feature_groups
    (
        attention_probabilities,
        losses,
        query_blocks,
        passage_blocks,
        inverses,
        fetched,
        wanted_table,
    ) = front(query_hidden, passage_hidden, head_weight, neg_blocks, pos_ids)
    all_wanted = wanted_table[:, :, 0].reshape(dp_count * request_count)
    losses = losses[:, 0]
    passage_inv = inverses[0, :4].reshape(row_count)
    query_inv = inverses[1, :4].reshape(row_count)
    query_unit = query_blocks.reshape(row_count, embed_width).astype(jnp.float32)
    passage_unit = passage_blocks.reshape(row_count, embed_width).astype(jnp.float32)
    retrieved_documents = jnp.concatenate(
        [passage_blocks[:, None], fetched.reshape(block_count, neg_count, block_rows, embed_width)],
        axis=1,
    ).reshape(block_count, cand_rows, embed_width)
    d_query = jnp.einsum(
        "bqc,bce->bqe",
        attention_probabilities,
        retrieved_documents,
        preferred_element_type=jnp.float32,
    ).reshape(row_count, embed_width)
    d_cand = jnp.einsum(
        "bqc,bqe->bce", attention_probabilities, query_blocks, preferred_element_type=jnp.float32
    )
    own_terms = d_cand[:, :block_rows]
    neg_terms = (
        d_cand[:, block_rows:].reshape(request_count, block_rows, embed_width).astype(jnp.bfloat16)
    )
    outgoing = to_pieces(neg_terms, row_groups, feature_groups)
    returned = lax.all_to_all(outgoing, "dp", split_axis=0, concat_axis=0, tiled=True)
    selector = (
        all_wanted[None, :] == jnp.arange(total_blocks, dtype=jnp.int32)[:, None]
    ).astype(jnp.bfloat16)
    summed = jnp.dot(
        selector,
        returned.reshape(dp_count * request_count, piece_rows * piece_cols),
        preferred_element_type=jnp.float32,
    ).astype(jnp.bfloat16)
    summed = summed.reshape(dp_count, block_count, piece_rows, piece_cols)
    home = lax.all_to_all(summed, "dp", split_axis=0, concat_axis=0, tiled=True)
    d_passage = own_terms + from_pieces(home, row_groups, feature_groups).astype(jnp.float32)
    d_passage = d_passage.reshape(row_count, embed_width)
    query_inner = lax.psum(jnp.sum(query_unit * d_query, axis=1), "mp")
    passage_inner = lax.psum(jnp.sum(passage_unit * d_passage, axis=1), "mp")
    d_query_embed = back_norm(query_inv, query_unit, d_query, query_inner)
    d_passage_embed = back_norm(passage_inv, passage_unit, d_passage, passage_inner)
    query_grad = hidden_grad(d_query_embed, head_weight)
    grad_weight, passage_grad = tail(
        d_query_embed, d_passage_embed, query_hidden, passage_hidden, head_weight
    )
    return (
        losses.reshape(row_count),
        grad_weight,
        query_grad,
        passage_grad,
    )


def solution(mesh):
    placed = (P("dp", None), P("dp", None), P(None, "mp"), P("dp", None), P("dp"))
    return jax.shard_map(
        local,
        mesh=mesh,
        in_specs=placed,
        out_specs=(P("dp"), P("dp", "mp"), P("dp", "mp"), P("dp", "mp")),
        check_vma=False,
    )
```

```python
import jax
import jax.numpy as jnp
from jax import lax
from jax.experimental import pallas as pl
from jax.experimental.pallas import tpu as pltpu
from jax.sharding import PartitionSpec as P

logit_divisor = 0.02
epsilon = 1e-06


MESH = pl.DeviceIdType.MESH
ROW_CONTRACT = (((0,), (0,)), ((), ()))
COL_CONTRACT = (((1,), (1,)), ((), ()))
VMEM_LIMIT = 66 * 1024 * 1024 - 4 * 1024 * 1024


def greet(partners):
    barrier = pltpu.get_barrier_semaphore()
    for partner in partners:
        pl.semaphore_signal(barrier, 1, device_id=partner, device_id_type=MESH)
    pl.semaphore_wait(barrier, len(partners))


def remote(src, dst, send_sem, recv_sem, partner):
    return pltpu.make_async_remote_copy(
        src_ref=src,
        dst_ref=dst,
        send_sem=send_sem,
        recv_sem=recv_sem,
        device_id=partner,
        device_id_type=MESH,
    )


def depth_partner(k):
    return {"mp": lax.rem(lax.axis_index("mp") + k, 4)}


def head_load(head_hbm, head, load_sem, k):
    width = head.shape[1]
    owner = lax.rem(lax.axis_index("mp") + k, 4)
    return pltpu.make_async_copy(
        head_hbm.at[pl.ds(pl.multiple_of(owner * width, width), width)], head.at[k], load_sem.at[k]
    )


def hidden_send(part, landed, send_sem, recv_sem, k):
    return remote(
        part.at[k], landed.at[k - 1], send_sem.at[k - 1], recv_sem.at[k - 1], depth_partner(k)
    )


DEPTH_ORDER = (2, 1, 3, 0)


def hidden_parts(grad, head_hbm, head, part, landed, load_sem, send_sem, recv_sem):
    for k in DEPTH_ORDER:
        head_load(head_hbm, head, load_sem, k).wait()
        half = grad.shape[0] // 2

        @pl.loop(0, 2)
        def _(i):
            rows = pl.ds(pl.multiple_of(i * half, half), half)
            part[k, rows] = lax.dot_general(
                grad[rows], head[k], COL_CONTRACT, preferred_element_type=jnp.float32
            ).astype(jnp.bfloat16)

        if k:
            hidden_send(part, landed, send_sem, recv_sem, k).start()


def hidden_sum(part, landed, send_sem, recv_sem, out):
    for k in (1, 3, 2):
        hidden_send(part, landed, send_sem, recv_sem, k).wait_recv()
    rows_step = 64

    @pl.loop(0, out.shape[0] // rows_step)
    def _(i):
        rows = pl.ds(pl.multiple_of(i * rows_step, rows_step), rows_step)
        total = part[0, rows].astype(jnp.float32)
        for k in range(3):
            total = total + landed[k, rows].astype(jnp.float32)
        out[rows] = total.astype(jnp.bfloat16)

    for k in (1, 3, 2):
        hidden_send(part, landed, send_sem, recv_sem, k).wait_send()


def place():
    dp = lax.axis_index("dp")
    return lax.div(dp, 8), lax.rem(lax.div(dp, 2), 4), lax.rem(dp, 2)


def at(y, x, core):
    return {"dp": y * 8 + x * 2 + core}


OFFSETS = tuple(
    (dy, dx, core)
    for dy, dx in (
        (2, 2), (1, 3), (3, 1), (1, 1), (3, 3), (0, 2), (2, 0), (1, 2),
        (3, 2), (2, 1), (2, 3), (0, 1), (1, 0), (0, 3), (3, 0), (0, 0),
    )
    for core in range(2)
    if dy or dx or core
)


def plane_peer(offset):
    y, x, core = place()
    return (
        lax.rem(y + offset[0], 4) * 8 + lax.rem(x + offset[1], 4) * 2 + lax.rem(core + offset[2], 2)
    )


def share_rows(device):
    return pl.ds(pl.multiple_of(lax.div(device, 4) * 16, 16), 16)


def share_cols(device):
    return pl.ds(pl.multiple_of(lax.rem(device, 4) * 256, 256), 256)


def diagonal():
    rows = lax.broadcasted_iota(jnp.int32, (128, 128), 0)
    return rows == lax.broadcasted_iota(jnp.int32, (128, 128), 1)


def as_row(column):
    spread = jnp.broadcast_to(column, (128, 128))
    return jnp.sum(jnp.where(diagonal(), spread, 0.0), axis=0, keepdims=True)


def as_column(row):
    spread = jnp.broadcast_to(row, (128, 128))
    return jnp.sum(jnp.where(diagonal(), spread, 0.0), axis=1, keepdims=True)


def depth_copy(src, dst, send_sem, recv_sem, k):
    return remote(src, dst.at[k - 1], send_sem.at[k - 1], recv_sem.at[k - 1], depth_partner(k))


def depth_start(src, dst, send_sem, recv_sem):
    for k in (2, 1, 3):
        depth_copy(src, dst, send_sem, recv_sem, k).start()


def depth_total(src, dst, send_sem, recv_sem):
    for k in (1, 3, 2):
        depth_copy(src, dst, send_sem, recv_sem, k).wait_recv()
    return src[...] + dst[0] + dst[1] + dst[2]


def depth_finish(src, dst, send_sem, recv_sem):
    for k in (1, 2, 3):
        depth_copy(src, dst, send_sem, recv_sem, k).wait_send()


def back_kernel(
    weights,
    query_norm,
    passage_norm,
    fetched,
    inverses,
    head_hbm,
    d_query_embed,
    own_terms,
    returned,
    hidden_out,
    head,
    d_query,
    outgoing,
    part,
    landed,
    inner,
    inner_in,
    load_sem,
    depth_send,
    depth_recv,
    return_send,
    return_recv,
    inner_send,
    inner_recv,
):
    dp = lax.axis_index("dp")
    width = head.shape[1]
    for k in DEPTH_ORDER:
        head_load(head_hbm, head, load_sem, k).start()
    greet(
        [{"dp": plane_peer(offset)} for offset in OFFSETS]
        + [depth_partner(k) for k in (1, 2, 3)]
    )

    @pl.loop(0, 4)
    def _(b):
        outgoing[pl.ds(b * 4, 4)] = (
            lax.dot_general(
                weights[b, :, 128:],
                query_norm[b],
                ROW_CONTRACT,
                preferred_element_type=jnp.float32,
            )
            .astype(jnp.bfloat16)
            .reshape(4, 128, width)
        )

    def return_copy(j):
        peer = plane_peer(OFFSETS[j])
        return remote(
            outgoing.at[:, share_rows(peer), share_cols(peer)],
            returned.at[dp],
            return_send.at[j],
            return_recv.at[j],
            {"dp": peer},
        )

    for j in range(31):
        return_copy(j).start()
    returned[dp] = outgoing[:, share_rows(dp), share_cols(dp)]
    inner[4:8] = jnp.zeros((4, 128), jnp.float32)

    for b in range(4):
        total = jnp.dot(
            weights[b, :, :128], passage_norm[b], preferred_element_type=jnp.float32
        ) + jnp.dot(
            weights[b, :, 128:],
            fetched[4 * b : 4 * b + 4].reshape(512, width),
            preferred_element_type=jnp.float32,
        )
        d_query[b] = total
        inner[b : b + 1] = as_row(
            jnp.sum(query_norm[b].astype(jnp.float32) * total, axis=1, keepdims=True)
        )
    inner_args = (inner, inner_in, inner_send, inner_recv)
    depth_start(*inner_args)

    @pl.loop(0, 4)
    def _(b):
        own_terms[b] = lax.dot_general(
            weights[b, :, :128], query_norm[b], ROW_CONTRACT, preferred_element_type=jnp.float32
        )

    total_inner = depth_total(*inner_args)
    for b in range(4):
        d_query_embed[b * 128 : (b + 1) * 128] = embed_grad(
            inverses[1, b : b + 1], query_norm[b], d_query[b], total_inner[b : b + 1]
        )
    hidden_parts(d_query_embed, head_hbm, head, part, landed, load_sem, depth_send, depth_recv)
    hidden_sum(part, landed, depth_send, depth_recv, hidden_out)
    for j in range(31):
        return_copy(j).wait_recv()
    depth_finish(*inner_args)
    for j in range(31):
        return_copy(j).wait_send()


def embed_grad(inverse_row, unit, d_unit, inner_row):
    return (
        as_column(inverse_row) * (d_unit - unit.astype(jnp.float32) * as_column(inner_row))
    ).astype(jnp.bfloat16)


def back(weights, query_norm, passage_norm, fetched, inverses, head_weight):
    bf16 = jnp.bfloat16
    f32 = jnp.float32
    width = head_weight.shape[1]
    vmem = pl.BlockSpec(memory_space=pltpu.VMEM)
    dma = pltpu.SemaphoreType.DMA
    return pl.pallas_call(
        back_kernel,
        out_shape=(
            jax.ShapeDtypeStruct((512, width), bf16),
            jax.ShapeDtypeStruct((4, 128, width), f32),
            jax.ShapeDtypeStruct((32, 16, 16, 256), bf16),
            jax.ShapeDtypeStruct((512, width), bf16),
        ),
        in_specs=[vmem] * 5 + [pl.BlockSpec(memory_space=pl.ANY)],
        out_specs=(vmem,) * 4,
        scratch_shapes=[
            pltpu.VMEM((4, width, width), bf16),
            pltpu.VMEM((4, 128, width), f32),
            pltpu.VMEM((16, 128, width), bf16),
            pltpu.VMEM((4, 512, width), bf16),
            pltpu.VMEM((3, 512, width), bf16),
            pltpu.VMEM((8, 128), f32),
            pltpu.VMEM((3, 8, 128), f32),
            dma((4,)),
            dma((3,)),
            dma((3,)),
            dma((31,)),
            dma((31,)),
            dma((3,)),
            dma((3,)),
        ],
        compiler_params=pltpu.CompilerParams(
            collective_id=1, has_side_effects=True, vmem_limit_bytes=VMEM_LIMIT
        ),
        name="back",
    )(weights, query_norm, passage_norm, fetched, inverses, head_weight)


def add_kernel(table, returned, out, total):
    total[...] = jnp.zeros_like(total)

    @pl.loop(0, 512, unroll=4)
    def _(i):
        block = table[i]
        total[block] += returned[i].astype(jnp.float32)

    out[...] = total[...].astype(jnp.bfloat16)


def add_returned(table, returned):
    vmem = pl.BlockSpec(memory_space=pltpu.VMEM)
    return pl.pallas_call(
        add_kernel,
        out_shape=jax.ShapeDtypeStruct((128, 16, 256), jnp.bfloat16),
        in_specs=[pl.BlockSpec(memory_space=pltpu.SMEM), vmem],
        out_specs=vmem,
        scratch_shapes=[pltpu.VMEM((128, 16, 256), jnp.float32)],
        name="add_returned",
    )(table, returned)


def tail_kernel(
    d_query,
    block_sums,
    own_terms,
    passage_norm,
    inverses,
    query_hbm,
    passage_hbm,
    head_hbm,
    weight_out,
    hidden_out,
    home,
    d_total,
    d_passage,
    inner,
    inner_in,
    home_send,
    home_recv,
    inner_send,
    inner_recv,
    head,
    query,
    passage,
    summed,
    sibling_in,
    pair,
    first_in,
    second_out,
    second_in,
    part,
    landed,
    load_sem,
    hidden_load_sem,
    depth_send,
    depth_recv,
    core_send,
    core_recv,
    first_send,
    first_recv,
    second_send,
    second_recv,
):
    y, x, core = place()
    wide = query.shape[1]
    rows = weight_out.shape[0]
    half = weight_out.shape[1] // 2

    def chunk_of(i):
        return lax.rem(y + 1 + lax.div(i, 2), 4) * 2 + lax.rem(lax.div(x, 2) + 1 + i, 2)

    def hidden_loads(i, slot):
        columns = pl.ds(pl.multiple_of(chunk_of(i) * wide, wide), wide)
        return (
            pltpu.make_async_copy(
                query_hbm.at[:, columns], query.at[slot], hidden_load_sem.at[0, slot]
            ),
            pltpu.make_async_copy(
                passage_hbm.at[:, columns], passage.at[slot], hidden_load_sem.at[1, slot]
            ),
        )

    for k in DEPTH_ORDER:
        head_load(head_hbm, head, load_sem, k).start()
    for copy in hidden_loads(0, 0) + hidden_loads(1, 1):
        copy.start()
    greet(
        [{"dp": plane_peer(offset)} for offset in OFFSETS]
        + [depth_partner(k) for k in (1, 2, 3)]
    )
    dp = lax.axis_index("dp")

    def home_copy(j):
        peer = plane_peer(OFFSETS[j])
        return remote(
            block_sums.at[pl.ds(peer * 4, 4)],
            home.at[:, share_rows(dp), share_cols(dp)],
            home_send.at[j],
            home_recv.at[j],
            {"dp": peer},
        )

    for j in range(31):
        home_copy(j).start()
    home[:, share_rows(dp), share_cols(dp)] = block_sums[pl.ds(dp * 4, 4)]
    inner[4:8] = jnp.zeros((4, 128), jnp.float32)
    for j in range(31):
        home_copy(j).wait_recv()
    for b in range(4):
        total = own_terms[b] + home[b].astype(jnp.float32)
        d_total[b] = total
        inner[b : b + 1] = as_row(
            jnp.sum(passage_norm[b].astype(jnp.float32) * total, axis=1, keepdims=True)
        )
    inner_args = (inner, inner_in, inner_send, inner_recv)
    depth_start(*inner_args)
    total_inner = depth_total(*inner_args)
    for b in range(4):
        d_passage[b * 128 : (b + 1) * 128] = embed_grad(
            inverses[0, b : b + 1], passage_norm[b], d_total[b], total_inner[b : b + 1]
        )
    hidden_parts(d_passage, head_hbm, head, part, landed, load_sem, depth_send, depth_recv)

    def core_copy(chip):
        return remote(
            summed.at[chip, 1 - core],
            sibling_in.at[chip],
            core_send.at[chip],
            core_recv.at[chip],
            at(y, x, 1 - core),
        )

    def first_x(chip):
        to_y, to_x = lax.div(chip, 4), lax.rem(chip, 4)
        k = lax.rem(to_x - x + 4, 4)
        slot = lax.rem(k + 3, 4)
        return k, remote(
            pair.at[chip, 0],
            first_in.at[0, slot, to_y],
            first_send.at[0, chip],
            first_recv.at[0, slot, to_y],
            at(y, to_x, core),
        )

    def first_y(chip):
        to_y, to_x = lax.div(chip, 4), lax.rem(chip, 4)
        k = lax.rem(to_y - y + 4, 4)
        slot = lax.rem(k + 3, 4)
        return k, remote(
            pair.at[chip, 1],
            first_in.at[1, slot, to_x],
            first_send.at[1, chip],
            first_recv.at[1, slot, to_x],
            at(to_y, x, core),
        )

    def produce(i):
        slot = lax.rem(i, 2)
        for copy in hidden_loads(i, slot):
            copy.wait()
        chunk = chunk_of(i)
        for j in range(2):
            columns = slice(j * 2 * rows, (j + 1) * 2 * rows)
            total = lax.dot_general(
                query[slot, :, columns], d_query[...], ROW_CONTRACT, preferred_element_type=jnp.float32
            ) + lax.dot_general(
                passage[slot, :, columns],
                d_passage[...],
                ROW_CONTRACT,
                preferred_element_type=jnp.float32,
            )
            summed[chunk * 2 + j] = total.astype(jnp.bfloat16).reshape(2, rows, 2 * half)
            core_copy(chunk * 2 + j).start()

        @pl.when(i < 6)
        def _():
            for copy in hidden_loads(i + 2, slot):
                copy.start()

    def combine(i):
        for j in range(2):
            chip = chunk_of(i) * 2 + j
            core_copy(chip).wait_recv()
            total = (
                summed[chip, core].astype(jnp.float32) + sibling_in[chip].astype(jnp.float32)
            ).astype(jnp.bfloat16)
            pair[chip, 0] = total[:, :half]
            pair[chip, 1] = total[:, half:]
            for first in (first_x, first_y):
                k, copy = first(chip)

                @pl.when(k != 0)
                def _():
                    copy.start()

    @pl.loop(0, 9)
    def _(i):
        @pl.when(i < 8)
        def _():
            produce(i)

        @pl.when(i > 0)
        def _():
            combine(i - 1)

    def first_arrival(side, k, other):
        return remote(
            first_in.at[side, k, other],
            first_in.at[side, k, other],
            first_send.at[side, 0],
            first_recv.at[side, k, other],
            at(y, x, 1 - core),
        )

    def gathered(side, other):
        chip = other * 4 + x if side == 0 else y * 4 + other
        total = pair[chip, side].astype(jnp.float32)
        for k in range(3):
            first_arrival(side, k, other).wait_recv()
            total = total + first_in[side, k, other].astype(jnp.float32)
        return total

    def second_copy(side, k):
        if side == 0:
            partner = at(lax.rem(y + k, 4), x, core)
        else:
            partner = at(y, lax.rem(x + k, 4), core)
        return remote(
            second_out.at[side, k - 1],
            second_in.at[side, k - 1],
            second_send.at[side, k - 1],
            second_recv.at[side, k - 1],
            partner,
        )

    for k in (1, 2, 3):
        for side in range(2):
            base = y if side == 0 else x
            second_out[side, k - 1] = gathered(side, lax.rem(base + k, 4)).astype(jnp.bfloat16)
            second_copy(side, k).start()
    for side in range(2):
        weight_out[:, side * half : (side + 1) * half] = gathered(side, y if side == 0 else x)
    for side in range(2):
        for k in (1, 2, 3):
            second_copy(side, k).wait_recv()
            weight_out[:, side * half : (side + 1) * half] += second_in[side, k - 1].astype(
                jnp.float32
            )
    hidden_sum(part, landed, depth_send, depth_recv, hidden_out)
    for j in range(31):
        home_copy(j).wait_send()
    depth_finish(*inner_args)

    @pl.loop(0, 16)
    def _(chip):
        core_copy(chip).wait_send()
        for first in (first_x, first_y):
            k, copy = first(chip)

            @pl.when(k != 0)
            def _():
                copy.wait_send()

    for side in range(2):
        for k in (1, 2, 3):
            second_copy(side, k).wait_send()


def tail(
    d_query,
    block_sums,
    own_terms,
    passage_norm,
    inverses,
    query_hidden,
    passage_hidden,
    head_weight,
):
    rows, width = d_query.shape
    hidden = head_weight.shape[0]
    share = hidden // 32
    bf16 = jnp.bfloat16
    vmem = pl.BlockSpec(memory_space=pltpu.VMEM)
    hbm = pl.BlockSpec(memory_space=pl.ANY)
    dma = pltpu.SemaphoreType.DMA
    return pl.pallas_call(
        tail_kernel,
        out_shape=(
            jax.ShapeDtypeStruct((share, width), jnp.float32),
            jax.ShapeDtypeStruct((rows, width), bf16),
        ),
        in_specs=[vmem] * 5 + [hbm] * 3,
        out_specs=(vmem, vmem),
        scratch_shapes=[
            pltpu.VMEM((4, 128, width), bf16),
            pltpu.VMEM((4, 128, width), jnp.float32),
            pltpu.VMEM((rows, width), bf16),
            pltpu.VMEM((8, 128), jnp.float32),
            pltpu.VMEM((3, 8, 128), jnp.float32),
            dma((31,)),
            dma((31,)),
            dma((3,)),
            dma((3,)),
            pltpu.VMEM((4, width, width), bf16),
            pltpu.VMEM((2, rows, 4 * share), bf16),
            pltpu.VMEM((2, rows, 4 * share), bf16),
            pltpu.VMEM((16, 2, share, width), bf16),
            pltpu.VMEM((16, share, width), bf16),
            pltpu.VMEM((16, 2, share, width // 2), bf16),
            pltpu.VMEM((2, 3, 4, share, width // 2), bf16),
            pltpu.VMEM((2, 3, share, width // 2), bf16),
            pltpu.VMEM((2, 3, share, width // 2), bf16),
            pltpu.VMEM((4, rows, width), bf16),
            pltpu.VMEM((3, rows, width), bf16),
            dma((4,)),
            dma((2, 2)),
            dma((3,)),
            dma((3,)),
            dma((16,)),
            dma((16,)),
            dma((2, 16)),
            dma((2, 3, 4)),
            dma((2, 3)),
            dma((2, 3)),
        ],
        compiler_params=pltpu.CompilerParams(
            collective_id=2, has_side_effects=True, vmem_limit_bytes=VMEM_LIMIT
        ),
        name="tail",
    )(
        d_query,
        block_sums,
        own_terms,
        passage_norm,
        inverses,
        query_hidden,
        passage_hidden,
        head_weight,
    )


def front_kernel(
    query_hbm,
    passage_hbm,
    head_hbm,
    wanted,
    positions,
    weights,
    losses,
    query_norm,
    passage_norm,
    inverses,
    fetched,
    all_wanted,
    head,
    hidden,
    embed,
    held,
    reply,
    partial,
    partial_in,
    squares,
    squares_in,
    table,
    load_sem,
    table_sem,
    square_send,
    square_recv,
    want_send,
    want_recv,
    spread_send,
    spread_recv,
    reply_send,
    reply_recv,
    partial_send,
    partial_recv,
    weight_send,
    weight_recv,
    loss_send,
    loss_recv,
):
    dp = lax.axis_index("dp")
    mp = lax.axis_index("mp")
    depth = head.shape[1]
    hidden_hbm = (passage_hbm, query_hbm)

    def hidden_load(side, chunk):
        columns = pl.ds(pl.multiple_of(chunk * depth, depth), depth)
        return pltpu.make_async_copy(
            hidden_hbm[side].at[:, columns], hidden.at[side, chunk], load_sem.at[side, chunk]
        )

    def head_chunk(chunk):
        rows = pl.ds(pl.multiple_of(chunk * depth, depth), depth)
        return pltpu.make_async_copy(head_hbm.at[rows], head.at[chunk], load_sem.at[2, chunk])

    for chunk in range(4):
        hidden_load(0, chunk).start()
        head_chunk(chunk).start()
    for chunk in range(4):
        hidden_load(1, chunk).start()
    embed[...] = jnp.zeros_like(embed)
    greet(
        [{"dp": plane_peer(offset)} for offset in OFFSETS]
        + [depth_partner(k) for k in (1, 2, 3)]
    )

    def want_copy(j):
        return remote(
            wanted,
            all_wanted.at[dp],
            want_send.at[j],
            want_recv.at[j],
            {"dp": plane_peer(OFFSETS[j])},
        )

    for j in range(31):
        want_copy(j).start()
    all_wanted[dp] = wanted[...]

    def project(side):
        @pl.loop(0, 4)
        def _(chunk):
            hidden_load(side, chunk).wait()
            if side == 0:
                head_chunk(chunk).wait()

            @pl.loop(0, 2)
            def _(i):
                rows = pl.ds(pl.multiple_of(i * 256, 256), 256)
                embed[side, rows] += jnp.dot(
                    hidden[side, chunk, rows], head[chunk], preferred_element_type=jnp.float32
                )

        for b in range(4):
            block = embed[side, b * 128 : (b + 1) * 128]
            squares[side, b : b + 1] = as_row(jnp.sum(block * block, axis=1, keepdims=True))
        squares[side, 4:8] = jnp.zeros((4, 128), jnp.float32)

    def square_args(side):
        return squares.at[side], squares_in.at[side], square_send.at[side], square_recv.at[side]

    def normalize(side, out):
        inverses[side] = lax.rsqrt(depth_total(*square_args(side)) + epsilon)
        for b in range(4):
            inverse = as_column(inverses[side, b : b + 1])
            out[b] = (embed[side, b * 128 : (b + 1) * 128] * inverse).astype(jnp.bfloat16)

    project(0)
    depth_start(*square_args(0))
    normalize(0, passage_norm)

    def spread_copy(j):
        peer = plane_peer(OFFSETS[j])
        return remote(
            passage_norm.at[:, share_rows(peer), share_cols(peer)],
            held.at[pl.ds(dp * 4, 4)],
            spread_send.at[j],
            spread_recv.at[j],
            {"dp": peer},
        )

    for j in range(31):
        spread_copy(j).start()
    for b in range(4):
        held[dp * 4 + b] = passage_norm[b, share_rows(dp), share_cols(dp)]
    project(1)
    depth_start(*square_args(1))
    normalize(1, query_norm)
    for j in range(31):
        want_copy(j).wait_recv()
    table_copy = pltpu.make_async_copy(all_wanted, table, table_sem)
    table_copy.start()
    table_copy.wait()
    for j in range(31):
        spread_copy(j).wait_recv()

    def reply_copy(j):
        peer = plane_peer(OFFSETS[j])
        return remote(
            reply.at[peer],
            fetched.at[:, share_rows(dp), share_cols(dp)],
            reply_send.at[j],
            reply_recv.at[j],
            {"dp": peer},
        )

    def gather(device):
        @pl.loop(0, 16, unroll=4)
        def _(i):
            reply[device, i] = held[table[device, i, 0]]

    for j in range(31):
        gather(plane_peer(OFFSETS[j]))
        reply_copy(j).start()
    gather(dp)
    fetched[:, share_rows(dp), share_cols(dp)] = reply[dp]
    for j in range(31):
        reply_copy(j).wait_recv()

    def partial_copy(k):
        return depth_copy(
            partial.at[lax.rem(mp + k, 4)], partial_in, partial_send, partial_recv, k
        )

    for k in DEPTH_ORDER:
        b = lax.rem(mp + k, 4)
        rows = query_norm[b]
        partial[b, :, :128] = lax.dot_general(
            rows, passage_norm[b], COL_CONTRACT, preferred_element_type=jnp.float32
        ).astype(jnp.bfloat16)
        others = fetched[pl.ds(b * 4, 4)].reshape(512, depth)
        partial[b, :, 128:] = lax.dot_general(
            rows, others, COL_CONTRACT, preferred_element_type=jnp.float32
        ).astype(jnp.bfloat16)
        if k:
            partial_copy(k).start()
    scores = partial[mp].astype(jnp.float32)
    for k in (1, 3, 2):
        partial_copy(k).wait_recv()
        scores = scores + partial_in[k - 1].astype(jnp.float32)
    scores = scores / logit_divisor
    columns = lax.broadcasted_iota(jnp.int32, scores.shape, 1).astype(jnp.float32)
    matching = (columns == as_column(positions[pl.ds(mp, 1)])).astype(jnp.float32)
    powers = jnp.exp(scores)
    totals = jnp.sum(powers, axis=1, keepdims=True)
    loss = jnp.log(totals) - jnp.sum(scores * matching, axis=1, keepdims=True)
    weights[mp] = ((powers / totals - matching) / logit_divisor).astype(jnp.bfloat16)
    losses[mp] = jnp.broadcast_to(as_row(loss), (8, 128))

    def weight_copies(k):
        return (
            remote(
                weights.at[mp],
                weights.at[mp],
                weight_send.at[k - 1],
                weight_recv.at[k - 1],
                depth_partner(k),
            ),
            remote(
                losses.at[mp],
                losses.at[mp],
                loss_send.at[k - 1],
                loss_recv.at[k - 1],
                depth_partner(k),
            ),
        )

    for k in (2, 1, 3):
        for copy in weight_copies(k):
            copy.start()
    for j in range(31):
        want_copy(j).wait_send()
        spread_copy(j).wait_send()
        reply_copy(j).wait_send()
    depth_finish(*square_args(0))
    depth_finish(*square_args(1))
    for k in (1, 3, 2):
        partial_copy(k).wait_send()
        for copy in weight_copies(k):
            copy.wait()


def front(query_hidden, passage_hidden, head_weight, neg_blocks, pos_ids):
    bf16 = jnp.bfloat16
    f32 = jnp.float32
    rows = query_hidden.shape[0]
    width = head_weight.shape[1]
    wanted = jnp.broadcast_to(neg_blocks.reshape(16, 1), (16, 128))
    positions = pos_ids.reshape(4, 128).astype(f32)
    vmem = pl.BlockSpec(memory_space=pltpu.VMEM)
    hbm = pl.BlockSpec(memory_space=pl.ANY)
    dma = pltpu.SemaphoreType.DMA
    return pl.pallas_call(
        front_kernel,
        out_shape=(
            jax.ShapeDtypeStruct((4, 128, 640), bf16),
            jax.ShapeDtypeStruct((4, 8, 128), f32),
            jax.ShapeDtypeStruct((4, 128, width), bf16),
            jax.ShapeDtypeStruct((4, 128, width), bf16),
            jax.ShapeDtypeStruct((2, 8, 128), f32),
            jax.ShapeDtypeStruct((16, 128, width), bf16),
            jax.ShapeDtypeStruct((32, 16, 128), jnp.int32),
        ),
        in_specs=[hbm, hbm, hbm, vmem, vmem],
        out_specs=(vmem,) * 7,
        scratch_shapes=[
            pltpu.VMEM((4, width, width), bf16),
            pltpu.VMEM((2, 4, rows, width), bf16),
            pltpu.VMEM((2, rows, width), f32),
            pltpu.VMEM((128, 16, 256), bf16),
            pltpu.VMEM((32, 16, 16, 256), bf16),
            pltpu.VMEM((4, 128, 640), bf16),
            pltpu.VMEM((3, 128, 640), bf16),
            pltpu.VMEM((2, 8, 128), f32),
            pltpu.VMEM((2, 3, 8, 128), f32),
            pltpu.SMEM((32, 16, 128), jnp.int32),
            dma((3, 4)),
            dma,
            dma((2, 3)),
            dma((2, 3)),
            dma((31,)),
            dma((31,)),
            dma((31,)),
            dma((31,)),
            dma((31,)),
            dma((31,)),
            dma((3,)),
            dma((3,)),
            dma((3,)),
            dma((3,)),
            dma((3,)),
            dma((3,)),
        ],
        compiler_params=pltpu.CompilerParams(
            collective_id=3, has_side_effects=True, vmem_limit_bytes=VMEM_LIMIT
        ),
        name="front",
    )(query_hidden, passage_hidden, head_weight, wanted, positions)


def local(query_hidden, passage_hidden, head_weight, neg_blocks, pos_ids):
    weights, losses, query_norm, passage_norm, inverses, fetched, table = front(
        query_hidden, passage_hidden, head_weight, neg_blocks, pos_ids
    )
    d_query, own_terms, returned, query_grad = back(
        weights, query_norm, passage_norm, fetched, inverses, head_weight
    )
    block_sums = add_returned(table[:, :, 0].reshape(512), returned.reshape(512, 16, 256))
    grad_weight, passage_grad = tail(
        d_query,
        block_sums,
        own_terms,
        passage_norm,
        inverses,
        query_hidden,
        passage_hidden,
        head_weight,
    )
    return losses[:, 0].reshape(512), grad_weight, query_grad, passage_grad


def solution(mesh):
    placed = (P("dp", None), P("dp", None), P(None, "mp"), P("dp", None), P("dp"))
    return jax.shard_map(
        local,
        mesh=mesh,
        in_specs=placed,
        out_specs=(P("dp"), P("dp", "mp"), P("dp", "mp"), P("dp", "mp")),
        check_vma=False,
    )
```

```python
import jax
import jax.numpy as jnp
from jax import lax
from jax.experimental import pallas as pl
from jax.experimental.pallas import tpu as pltpu
from jax.sharding import PartitionSpec as P

logit_divisor = 0.02
epsilon = 1e-06


MESH = pl.DeviceIdType.MESH
ROW_CONTRACT = (((0,), (0,)), ((), ()))
COL_CONTRACT = (((1,), (1,)), ((), ()))
VMEM_LIMIT = 66 * 1024 * 1024 - 4 * 1024 * 1024


def greet(partners):
    barrier = pltpu.get_barrier_semaphore()
    for partner in partners:
        pl.semaphore_signal(barrier, 1, device_id=partner, device_id_type=MESH)
    pl.semaphore_wait(barrier, len(partners))


def remote(src, dst, send_sem, recv_sem, partner):
    return pltpu.make_async_remote_copy(
        src_ref=src,
        dst_ref=dst,
        send_sem=send_sem,
        recv_sem=recv_sem,
        device_id=partner,
        device_id_type=MESH,
    )


def depth_partner(k):
    return {"mp": lax.rem(lax.axis_index("mp") + k, 4)}


def head_load(head_hbm, head, load_sem, k):
    width = head.shape[1]
    owner = lax.rem(lax.axis_index("mp") + k, 4)
    return pltpu.make_async_copy(
        head_hbm.at[pl.ds(pl.multiple_of(owner * width, width), width)], head.at[k], load_sem.at[k]
    )


def hidden_send(part, early_in, final_in, send_sem, recv_sem, side, stage):
    half = part.shape[1] // 2
    merged_rows = pl.ds(side * half, half)
    plain_rows = pl.ds((1 - side) * half, half)
    near = (1, 3)[side]
    if stage == 0:
        src, dst = part.at[2, merged_rows], early_in.at[side]
    elif stage == 1:
        src, dst = part.at[near, plain_rows], final_in.at[side, plain_rows]
    else:
        src, dst = part.at[near, merged_rows], final_in.at[side, merged_rows]
    return remote(src, dst, send_sem.at[side, stage], recv_sem.at[side, stage], depth_partner(near))


DEPTH_ORDER = (2, 1, 3, 0)


def hidden_parts(grad, head_of, part, early_in, final_in, send_sem, recv_sem):
    half = grad.shape[0] // 2
    sends = (part, early_in, final_in, send_sem, recv_sem)
    for k in DEPTH_ORDER:
        head = head_of(k)

        @pl.loop(0, 2)
        def _(i):
            rows = pl.ds(pl.multiple_of(i * half, half), half)
            part[k, rows] = lax.dot_general(
                grad[rows], head[...], COL_CONTRACT, preferred_element_type=jnp.float32
            ).astype(jnp.bfloat16)

        if k == 2:
            hidden_send(*sends, 0, 0).start()
            hidden_send(*sends, 1, 0).start()
        elif k:
            hidden_send(*sends, k // 2, 1).start()


def hidden_merge(part, early_in, final_in, send_sem, recv_sem):
    half = part.shape[1] // 2
    step = 64
    for side in range(2):
        hidden_send(part, early_in, final_in, send_sem, recv_sem, side, 0).wait_recv()
        near = (1, 3)[side]

        @pl.loop(0, half // step)
        def _(i):
            rows = pl.ds(pl.multiple_of(side * half + i * step, step), step)
            early_rows = pl.ds(pl.multiple_of(i * step, step), step)
            part[near, rows] = (
                part[near, rows].astype(jnp.float32)
                + early_in[side, early_rows].astype(jnp.float32)
            ).astype(jnp.bfloat16)

        hidden_send(part, early_in, final_in, send_sem, recv_sem, side, 2).start()


def hidden_sum(part, early_in, final_in, send_sem, recv_sem, out):
    step = 64
    sends = (part, early_in, final_in, send_sem, recv_sem)
    for stage in (1, 2):
        for side in range(2):
            hidden_send(*sends, side, stage).wait_recv()

    @pl.loop(0, out.shape[0] // step)
    def _(i):
        rows = pl.ds(pl.multiple_of(i * step, step), step)
        out[rows] = (
            part[0, rows].astype(jnp.float32)
            + final_in[0, rows].astype(jnp.float32)
            + final_in[1, rows].astype(jnp.float32)
        ).astype(jnp.bfloat16)

    for stage in range(3):
        for side in range(2):
            hidden_send(*sends, side, stage).wait_send()


def place():
    dp = lax.axis_index("dp")
    return lax.div(dp, 8), lax.rem(lax.div(dp, 2), 4), lax.rem(dp, 2)


def at(y, x, core):
    return {"dp": y * 8 + x * 2 + core}


OFFSETS = tuple(
    (dy, dx, core)
    for dy, dx in (
        (2, 2), (1, 3), (3, 1), (1, 1), (3, 3), (0, 2), (2, 0), (1, 2),
        (3, 2), (2, 1), (2, 3), (0, 1), (1, 0), (0, 3), (3, 0), (0, 0),
    )
    for core in range(2)
    if dy or dx or core
)


def plane_peer(offset):
    y, x, core = place()
    return (
        lax.rem(y + offset[0], 4) * 8 + lax.rem(x + offset[1], 4) * 2 + lax.rem(core + offset[2], 2)
    )


def share_rows(device):
    return pl.ds(pl.multiple_of(lax.div(device, 4) * 16, 16), 16)


def share_cols(device):
    return pl.ds(pl.multiple_of(lax.rem(device, 4) * 256, 256), 256)


def diagonal():
    rows = lax.broadcasted_iota(jnp.int32, (128, 128), 0)
    return rows == lax.broadcasted_iota(jnp.int32, (128, 128), 1)


def as_row(column):
    spread = jnp.broadcast_to(column, (128, 128))
    return jnp.sum(jnp.where(diagonal(), spread, 0.0), axis=0, keepdims=True)


def as_column(row):
    spread = jnp.broadcast_to(row, (128, 128))
    return jnp.sum(jnp.where(diagonal(), spread, 0.0), axis=1, keepdims=True)


def depth_copy(src, dst, send_sem, recv_sem, k):
    return remote(src, dst.at[k - 1], send_sem.at[k - 1], recv_sem.at[k - 1], depth_partner(k))


def depth_start(src, dst, send_sem, recv_sem):
    for k in (2, 1, 3):
        depth_copy(src, dst, send_sem, recv_sem, k).start()


def depth_total(src, dst, send_sem, recv_sem):
    for k in (1, 3, 2):
        depth_copy(src, dst, send_sem, recv_sem, k).wait_recv()
    return src[...] + dst[0] + dst[1] + dst[2]


def depth_finish(src, dst, send_sem, recv_sem):
    for k in (1, 2, 3):
        depth_copy(src, dst, send_sem, recv_sem, k).wait_send()


def embed_grad(inverse_row, unit, d_unit, inner_row):
    return (
        as_column(inverse_row) * (d_unit - unit.astype(jnp.float32) * as_column(inner_row))
    ).astype(jnp.bfloat16)


def add_kernel(table, returned, out, total):
    total[...] = jnp.zeros_like(total)

    @pl.loop(0, 512, unroll=4)
    def _(i):
        block = table[i]
        total[block] += returned[i].astype(jnp.float32)

    out[...] = total[...].astype(jnp.bfloat16)


def add_returned(table, returned):
    vmem = pl.BlockSpec(memory_space=pltpu.VMEM)
    return pl.pallas_call(
        add_kernel,
        out_shape=jax.ShapeDtypeStruct((128, 16, 256), jnp.bfloat16),
        in_specs=[pl.BlockSpec(memory_space=pltpu.SMEM), vmem],
        out_specs=vmem,
        scratch_shapes=[pltpu.VMEM((128, 16, 256), jnp.float32)],
        name="add_returned",
    )(table, returned)


def tail_kernel(
    d_query,
    block_sums,
    own_terms,
    passage_norm,
    inverses,
    query_hbm,
    passage_hbm,
    head_hbm,
    weight_out,
    hidden_out,
    home,
    d_total,
    d_passage,
    inner,
    inner_in,
    home_send,
    home_recv,
    inner_send,
    inner_recv,
    head,
    query,
    passage,
    summed,
    sibling_in,
    pair,
    first_in,
    second_out,
    second_in,
    part,
    early_in,
    final_in,
    load_sem,
    hidden_load_sem,
    depth_send,
    depth_recv,
    core_send,
    core_recv,
    first_send,
    first_recv,
    second_send,
    second_recv,
):
    y, x, core = place()
    wide = query.shape[1]
    rows = weight_out.shape[0]
    half = weight_out.shape[1] // 2

    def chunk_of(i):
        return lax.rem(y + 1 + lax.div(i, 2), 4) * 2 + lax.rem(lax.div(x, 2) + 1 + i, 2)

    def hidden_loads(i, slot):
        columns = pl.ds(pl.multiple_of(chunk_of(i) * wide, wide), wide)
        return (
            pltpu.make_async_copy(
                query_hbm.at[:, columns], query.at[slot], hidden_load_sem.at[0, slot]
            ),
            pltpu.make_async_copy(
                passage_hbm.at[:, columns], passage.at[slot], hidden_load_sem.at[1, slot]
            ),
        )

    for k in DEPTH_ORDER:
        head_load(head_hbm, head, load_sem, k).start()
    for copy in hidden_loads(0, 0) + hidden_loads(1, 1):
        copy.start()
    greet(
        [{"dp": plane_peer(offset)} for offset in OFFSETS]
        + [depth_partner(k) for k in (1, 2, 3)]
    )
    dp = lax.axis_index("dp")

    def home_copy(j):
        peer = plane_peer(OFFSETS[j])
        return remote(
            block_sums.at[pl.ds(peer * 4, 4)],
            home.at[:, share_rows(dp), share_cols(dp)],
            home_send.at[j],
            home_recv.at[j],
            {"dp": peer},
        )

    for j in range(31):
        home_copy(j).start()
    home[:, share_rows(dp), share_cols(dp)] = block_sums[pl.ds(dp * 4, 4)]
    inner[4:8] = jnp.zeros((4, 128), jnp.float32)
    for j in range(31):
        home_copy(j).wait_recv()
    for b in range(4):
        total = own_terms[b] + home[b].astype(jnp.float32)
        d_total[b] = total
        inner[b : b + 1] = as_row(
            jnp.sum(passage_norm[b].astype(jnp.float32) * total, axis=1, keepdims=True)
        )
    inner_args = (inner, inner_in, inner_send, inner_recv)
    depth_start(*inner_args)
    total_inner = depth_total(*inner_args)
    for b in range(4):
        d_passage[b * 128 : (b + 1) * 128] = embed_grad(
            inverses[0, b : b + 1], passage_norm[b], d_total[b], total_inner[b : b + 1]
        )
    for k in DEPTH_ORDER:
        head_load(head_hbm, head, load_sem, k).wait()
    depth_args = (part, early_in, final_in, depth_send, depth_recv)
    hidden_parts(d_passage, lambda k: head.at[k], *depth_args)

    def core_copy(chip):
        return remote(
            summed.at[chip, 1 - core],
            sibling_in.at[chip],
            core_send.at[chip],
            core_recv.at[chip],
            at(y, x, 1 - core),
        )

    def first_x(chip):
        to_y, to_x = lax.div(chip, 4), lax.rem(chip, 4)
        k = lax.rem(to_x - x + 4, 4)
        slot = lax.rem(k + 3, 4)
        return k, remote(
            pair.at[chip, 0],
            first_in.at[0, slot, to_y],
            first_send.at[0, chip],
            first_recv.at[0, slot, to_y],
            at(y, to_x, core),
        )

    def first_y(chip):
        to_y, to_x = lax.div(chip, 4), lax.rem(chip, 4)
        k = lax.rem(to_y - y + 4, 4)
        slot = lax.rem(k + 3, 4)
        return k, remote(
            pair.at[chip, 1],
            first_in.at[1, slot, to_x],
            first_send.at[1, chip],
            first_recv.at[1, slot, to_x],
            at(to_y, x, core),
        )

    def produce(i):
        slot = lax.rem(i, 2)
        for copy in hidden_loads(i, slot):
            copy.wait()
        chunk = chunk_of(i)
        for j in range(2):
            columns = slice(j * 2 * rows, (j + 1) * 2 * rows)
            total = lax.dot_general(
                query[slot, :, columns], d_query[...], ROW_CONTRACT, preferred_element_type=jnp.float32
            ) + lax.dot_general(
                passage[slot, :, columns],
                d_passage[...],
                ROW_CONTRACT,
                preferred_element_type=jnp.float32,
            )
            summed[chunk * 2 + j] = total.astype(jnp.bfloat16).reshape(2, rows, 2 * half)
            core_copy(chunk * 2 + j).start()

        @pl.when(i < 6)
        def _():
            for copy in hidden_loads(i + 2, slot):
                copy.start()

    def combine(i):
        for j in range(2):
            chip = chunk_of(i) * 2 + j
            core_copy(chip).wait_recv()
            total = (
                summed[chip, core].astype(jnp.float32) + sibling_in[chip].astype(jnp.float32)
            ).astype(jnp.bfloat16)
            pair[chip, 0] = total[:, :half]
            pair[chip, 1] = total[:, half:]
            for first in (first_x, first_y):
                k, copy = first(chip)

                @pl.when(k != 0)
                def _():
                    copy.start()

    @pl.loop(0, 9)
    def _(i):
        @pl.when(i == 4)
        def _():
            hidden_merge(*depth_args)

        @pl.when(i < 8)
        def _():
            produce(i)

        @pl.when(i > 0)
        def _():
            combine(i - 1)

    def first_arrival(side, k, other):
        return remote(
            first_in.at[side, k, other],
            first_in.at[side, k, other],
            first_send.at[side, 0],
            first_recv.at[side, k, other],
            at(y, x, 1 - core),
        )

    def gathered(side, other):
        chip = other * 4 + x if side == 0 else y * 4 + other
        total = pair[chip, side].astype(jnp.float32)
        for k in range(3):
            first_arrival(side, k, other).wait_recv()
            total = total + first_in[side, k, other].astype(jnp.float32)
        return total

    def second_copy(side, k):
        if side == 0:
            partner = at(lax.rem(y + k, 4), x, core)
        else:
            partner = at(y, lax.rem(x + k, 4), core)
        return remote(
            second_out.at[side, k - 1],
            second_in.at[side, k - 1],
            second_send.at[side, k - 1],
            second_recv.at[side, k - 1],
            partner,
        )

    for k in (1, 2, 3):
        for side in range(2):
            base = y if side == 0 else x
            second_out[side, k - 1] = gathered(side, lax.rem(base + k, 4)).astype(jnp.bfloat16)
            second_copy(side, k).start()
    for side in range(2):
        weight_out[:, side * half : (side + 1) * half] = gathered(side, y if side == 0 else x)
    for side in range(2):
        for k in (1, 2, 3):
            second_copy(side, k).wait_recv()
            weight_out[:, side * half : (side + 1) * half] += second_in[side, k - 1].astype(
                jnp.float32
            )
    hidden_sum(*depth_args, hidden_out)
    for j in range(31):
        home_copy(j).wait_send()
    depth_finish(*inner_args)

    @pl.loop(0, 16)
    def _(chip):
        core_copy(chip).wait_send()
        for first in (first_x, first_y):
            k, copy = first(chip)

            @pl.when(k != 0)
            def _():
                copy.wait_send()

    for side in range(2):
        for k in (1, 2, 3):
            second_copy(side, k).wait_send()


def tail(
    d_query,
    block_sums,
    own_terms,
    passage_norm,
    inverses,
    query_hidden,
    passage_hidden,
    head_weight,
):
    rows, width = d_query.shape
    hidden = head_weight.shape[0]
    share = hidden // 32
    bf16 = jnp.bfloat16
    vmem = pl.BlockSpec(memory_space=pltpu.VMEM)
    hbm = pl.BlockSpec(memory_space=pl.ANY)
    dma = pltpu.SemaphoreType.DMA
    return pl.pallas_call(
        tail_kernel,
        out_shape=(
            jax.ShapeDtypeStruct((share, width), jnp.float32),
            jax.ShapeDtypeStruct((rows, width), bf16),
        ),
        in_specs=[vmem] * 5 + [hbm] * 3,
        out_specs=(vmem, vmem),
        scratch_shapes=[
            pltpu.VMEM((4, 128, width), bf16),
            pltpu.VMEM((4, 128, width), jnp.float32),
            pltpu.VMEM((rows, width), bf16),
            pltpu.VMEM((8, 128), jnp.float32),
            pltpu.VMEM((3, 8, 128), jnp.float32),
            dma((31,)),
            dma((31,)),
            dma((3,)),
            dma((3,)),
            pltpu.VMEM((4, width, width), bf16),
            pltpu.VMEM((2, rows, 4 * share), bf16),
            pltpu.VMEM((2, rows, 4 * share), bf16),
            pltpu.VMEM((16, 2, share, width), bf16),
            pltpu.VMEM((16, share, width), bf16),
            pltpu.VMEM((16, 2, share, width // 2), bf16),
            pltpu.VMEM((2, 3, 4, share, width // 2), bf16),
            pltpu.VMEM((2, 3, share, width // 2), bf16),
            pltpu.VMEM((2, 3, share, width // 2), bf16),
            pltpu.VMEM((4, rows, width), bf16),
            pltpu.VMEM((2, rows // 2, width), bf16),
            pltpu.VMEM((2, rows, width), bf16),
            dma((4,)),
            dma((2, 2)),
            dma((2, 3)),
            dma((2, 3)),
            dma((16,)),
            dma((16,)),
            dma((2, 16)),
            dma((2, 3, 4)),
            dma((2, 3)),
            dma((2, 3)),
        ],
        compiler_params=pltpu.CompilerParams(
            collective_id=2, has_side_effects=True, vmem_limit_bytes=VMEM_LIMIT
        ),
        name="tail",
    )(
        d_query,
        block_sums,
        own_terms,
        passage_norm,
        inverses,
        query_hidden,
        passage_hidden,
        head_weight,
    )


def main_kernel(
    query_hbm,
    passage_hbm,
    head_hbm,
    negatives,
    positions,
    losses,
    passage_norm,
    inverses,
    table,
    d_query_embed,
    own_terms,
    returned,
    hidden_out,
    head,
    hidden,
    embed,
    query_norm,
    wanted,
    all_wanted,
    wanted_smem,
    targets,
    held,
    reply,
    fetched,
    partial,
    partial_in,
    weights,
    loss_rows,
    outgoing,
    part,
    early_in,
    final_in,
    squares,
    squares_in,
    load_sem,
    table_sem,
    square_send,
    square_recv,
    want_send,
    want_recv,
    spread_send,
    spread_recv,
    reply_send,
    reply_recv,
    return_send,
    return_recv,
    partial_send,
    partial_recv,
    weight_send,
    weight_recv,
    loss_send,
    loss_recv,
    depth_send,
    depth_recv,
):
    dp = lax.axis_index("dp")
    mp = lax.axis_index("mp")
    depth = head.shape[1]
    hidden_hbm = (passage_hbm, query_hbm)
    my_rows = pl.ds(pl.multiple_of(mp * 32, 32), 32)

    def hidden_load(side, chunk):
        columns = pl.ds(pl.multiple_of(chunk * depth, depth), depth)
        return pltpu.make_async_copy(
            hidden_hbm[side].at[:, columns], hidden.at[side, chunk], load_sem.at[side, chunk]
        )

    def head_chunk(chunk):
        rows = pl.ds(pl.multiple_of(chunk * depth, depth), depth)
        return pltpu.make_async_copy(head_hbm.at[rows], head.at[chunk], load_sem.at[2, chunk])

    for chunk in range(4):
        hidden_load(0, chunk).start()
        head_chunk(chunk).start()
    for chunk in range(4):
        hidden_load(1, chunk).start()
    for i in range(16):
        wanted[i : i + 1] = jnp.full((1, 128), negatives[i // 4, i % 4], jnp.int32)
    embed[...] = jnp.zeros_like(embed)
    greet(
        [{"dp": plane_peer(offset)} for offset in OFFSETS]
        + [depth_partner(k) for k in (1, 2, 3)]
    )

    def want_copy(j):
        return remote(
            wanted,
            all_wanted.at[dp],
            want_send.at[j],
            want_recv.at[j],
            {"dp": plane_peer(OFFSETS[j])},
        )

    for j in range(31):
        want_copy(j).start()
    all_wanted[dp] = wanted[...]
    for b in range(4):
        targets[b] = jnp.broadcast_to(as_column(positions[b : b + 1]), (128, 128))

    def project(side):
        @pl.loop(0, 4)
        def _(chunk):
            hidden_load(side, chunk).wait()
            if side == 0:
                head_chunk(chunk).wait()

            @pl.loop(0, 2)
            def _(i):
                rows = pl.ds(pl.multiple_of(i * 256, 256), 256)
                embed[side, rows] += jnp.dot(
                    hidden[side, chunk, rows], head[chunk], preferred_element_type=jnp.float32
                )

        for b in range(4):
            block = embed[side, b * 128 : (b + 1) * 128]
            squares[side, b : b + 1] = as_row(jnp.sum(block * block, axis=1, keepdims=True))
        squares[side, 4:8] = jnp.zeros((4, 128), jnp.float32)

    def square_args(side):
        return squares.at[side], squares_in.at[side], square_send.at[side], square_recv.at[side]

    def normalize(side, out):
        inverses[side] = lax.rsqrt(depth_total(*square_args(side)) + epsilon)
        for b in range(4):
            inverse = as_column(inverses[side, b : b + 1])
            out[b] = (embed[side, b * 128 : (b + 1) * 128] * inverse).astype(jnp.bfloat16)

    project(0)
    depth_start(*square_args(0))
    normalize(0, passage_norm)

    def spread_copy(j):
        peer = plane_peer(OFFSETS[j])
        return remote(
            passage_norm.at[:, share_rows(peer), share_cols(peer)],
            held.at[pl.ds(dp * 4, 4)],
            spread_send.at[j],
            spread_recv.at[j],
            {"dp": peer},
        )

    for j in range(31):
        spread_copy(j).start()
    for b in range(4):
        held[dp * 4 + b] = passage_norm[b, share_rows(dp), share_cols(dp)]
    project(1)
    depth_start(*square_args(1))
    normalize(1, query_norm)
    for j in range(31):
        want_copy(j).wait_recv()
    table_copy = pltpu.make_async_copy(all_wanted, wanted_smem, table_sem)
    table_copy.start()
    table_copy.wait()
    for j in range(31):
        spread_copy(j).wait_recv()

    def four(b):
        return pl.ds(b * 4, 4)

    def reply_copy(j, b):
        peer = plane_peer(OFFSETS[j])
        return remote(
            reply.at[peer, four(b)],
            fetched.at[four(b), share_rows(dp), share_cols(dp)],
            reply_send.at[j, b],
            reply_recv.at[j, b],
            {"dp": peer},
        )

    def gather(device, b):
        for i in range(4):
            reply[device, b * 4 + i] = held[wanted_smem[device, b * 4 + i, 0]]

    @pl.loop(0, 4)
    def _(b):
        for j in range(31):
            gather(plane_peer(OFFSETS[j]), b)
            reply_copy(j, b).start()
        gather(dp, b)
        fetched[four(b), share_rows(dp), share_cols(dp)] = reply[dp, four(b)]

    @pl.loop(0, 32)
    def _(device):
        for i in range(16):
            table[device * 16 + i] = wanted_smem[device, i, 0]

    def partial_copy(b, k):
        peer_rows = pl.ds(pl.multiple_of(lax.rem(mp + k, 4) * 32, 32), 32)
        return depth_copy(
            partial.at[b, peer_rows], partial_in.at[b], partial_send.at[b], partial_recv.at[b], k
        )

    def score(b):
        for j in range(31):
            reply_copy(j, b).wait_recv()
        rows = query_norm[b]
        partial[b, :, :128] = lax.dot_general(
            rows, passage_norm[b], COL_CONTRACT, preferred_element_type=jnp.float32
        ).astype(jnp.bfloat16)
        others = fetched[four(b)].reshape(512, depth)
        partial[b, :, 128:] = lax.dot_general(
            rows, others, COL_CONTRACT, preferred_element_type=jnp.float32
        ).astype(jnp.bfloat16)
        for k in (2, 1, 3):
            partial_copy(b, k).start()

    def weight_copy(b, k):
        return remote(
            weights.at[b, my_rows],
            weights.at[b, my_rows],
            weight_send.at[b, k - 1],
            weight_recv.at[b, k - 1],
            depth_partner(k),
        )

    def weigh(b):
        scores = partial[b, my_rows].astype(jnp.float32)
        for k in (1, 3, 2):
            partial_copy(b, k).wait_recv()
            scores = scores + partial_in[b, k - 1].astype(jnp.float32)
        scores = scores / logit_divisor
        columns = lax.broadcasted_iota(jnp.int32, scores.shape, 1).astype(jnp.float32)
        matching = (columns == targets[b, my_rows][:, :1]).astype(jnp.float32)
        powers = jnp.exp(scores)
        totals = jnp.sum(powers, axis=1, keepdims=True)
        loss = jnp.log(totals) - jnp.sum(scores * matching, axis=1, keepdims=True)
        weights[b, my_rows] = ((powers / totals - matching) / logit_divisor).astype(jnp.bfloat16)
        loss_rows[b, my_rows] = jnp.broadcast_to(loss, (32, 128))
        for k in (2, 1, 3):
            weight_copy(b, k).start()

    def return_copy(j, b):
        peer = plane_peer(OFFSETS[j])
        return remote(
            outgoing.at[four(b), share_rows(peer), share_cols(peer)],
            returned.at[dp, four(b)],
            return_send.at[j, b],
            return_recv.at[j, b],
            {"dp": peer},
        )

    def give_back(b):
        for k in (1, 3, 2):
            weight_copy(b, k).wait_recv()
        outgoing[four(b)] = (
            lax.dot_general(
                weights[b, :, 128:],
                query_norm[b],
                ROW_CONTRACT,
                preferred_element_type=jnp.float32,
            )
            .astype(jnp.bfloat16)
            .reshape(4, 128, depth)
        )
        for j in range(31):
            return_copy(j, b).start()
        returned[dp, four(b)] = outgoing[four(b), share_rows(dp), share_cols(dp)]
        total = jnp.dot(
            weights[b, :, :128], passage_norm[b], preferred_element_type=jnp.float32
        ) + jnp.dot(
            weights[b, :, 128:],
            fetched[four(b)].reshape(512, depth),
            preferred_element_type=jnp.float32,
        )
        embed[0, pl.ds(pl.multiple_of(b * 128, 128), 128)] = total
        squares[2, pl.ds(b, 1)] = as_row(
            jnp.sum(query_norm[b].astype(jnp.float32) * total, axis=1, keepdims=True)
        )
        own_terms[b] = lax.dot_general(
            weights[b, :, :128], query_norm[b], ROW_CONTRACT, preferred_element_type=jnp.float32
        )

    squares[2, 4:8] = jnp.zeros((4, 128), jnp.float32)

    @pl.loop(0, 6)
    def _(step):
        @pl.when(step < 4)
        def _():
            score(step)

        @pl.when((step >= 1) & (step < 5))
        def _():
            weigh(step - 1)

        @pl.when(step >= 2)
        def _():
            give_back(step - 2)

    depth_start(*square_args(2))

    def loss_copy(k):
        return remote(
            loss_rows.at[:, my_rows],
            loss_rows.at[:, my_rows],
            loss_send.at[k - 1],
            loss_recv.at[k - 1],
            depth_partner(k),
        )

    for k in (2, 1, 3):
        loss_copy(k).start()
    inner = depth_total(*square_args(2))
    for b in range(4):
        d_query_embed[b * 128 : (b + 1) * 128] = embed_grad(
            inverses[1, b : b + 1],
            query_norm[b],
            embed[0, b * 128 : (b + 1) * 128],
            inner[b : b + 1],
        )
    depth_args = (part, early_in, final_in, depth_send, depth_recv)
    hidden_parts(d_query_embed, lambda k: head.at[lax.rem(mp + k, 4)], *depth_args)
    for k in (1, 3, 2):
        loss_copy(k).wait_recv()
    for b in range(4):
        losses[b : b + 1] = as_row(loss_rows[b, :, :1])
    hidden_merge(*depth_args)
    for j in range(31):
        want_copy(j).wait_send()
        spread_copy(j).wait_send()
    for side in range(3):
        depth_finish(*square_args(side))
    for k in (1, 2, 3):
        loss_copy(k).wait_send()

    @pl.loop(0, 4)
    def _(b):
        for k in (1, 2, 3):
            partial_copy(b, k).wait_send()
            weight_copy(b, k).wait_send()
        for j in range(31):
            reply_copy(j, b).wait_send()
            return_copy(j, b).wait_send()
            return_copy(j, b).wait_recv()

    hidden_sum(*depth_args, hidden_out)


def main_part(query_hidden, passage_hidden, head_weight, neg_blocks, pos_ids):
    bf16 = jnp.bfloat16
    f32 = jnp.float32
    rows = query_hidden.shape[0]
    width = head_weight.shape[1]
    positions = pos_ids.reshape(4, 128).astype(f32)
    vmem = pl.BlockSpec(memory_space=pltpu.VMEM)
    smem = pl.BlockSpec(memory_space=pltpu.SMEM)
    hbm = pl.BlockSpec(memory_space=pl.ANY)
    dma = pltpu.SemaphoreType.DMA
    return pl.pallas_call(
        main_kernel,
        out_shape=(
            jax.ShapeDtypeStruct((4, 128), f32),
            jax.ShapeDtypeStruct((4, 128, width), bf16),
            jax.ShapeDtypeStruct((2, 8, 128), f32),
            jax.ShapeDtypeStruct((512,), jnp.int32),
            jax.ShapeDtypeStruct((rows, width), bf16),
            jax.ShapeDtypeStruct((4, 128, width), f32),
            jax.ShapeDtypeStruct((32, 16, 16, 256), bf16),
            jax.ShapeDtypeStruct((rows, width), bf16),
        ),
        in_specs=[hbm, hbm, hbm, smem, vmem],
        out_specs=(vmem, vmem, vmem, smem, vmem, vmem, vmem, vmem),
        scratch_shapes=[
            pltpu.VMEM((4, width, width), bf16),
            pltpu.VMEM((2, 4, rows, width), bf16),
            pltpu.VMEM((2, rows, width), f32),
            pltpu.VMEM((4, 128, width), bf16),
            pltpu.VMEM((16, 128), jnp.int32),
            pltpu.VMEM((32, 16, 128), jnp.int32),
            pltpu.SMEM((32, 16, 128), jnp.int32),
            pltpu.VMEM((4, 128, 128), f32),
            pltpu.VMEM((128, 16, 256), bf16),
            pltpu.VMEM((32, 16, 16, 256), bf16),
            pltpu.VMEM((16, 128, width), bf16),
            pltpu.VMEM((4, 128, 640), bf16),
            pltpu.VMEM((4, 3, 32, 640), bf16),
            pltpu.VMEM((4, 128, 640), bf16),
            pltpu.VMEM((4, 128, 128), f32),
            pltpu.VMEM((16, 128, width), bf16),
            pltpu.VMEM((4, rows, width), bf16),
            pltpu.VMEM((2, rows // 2, width), bf16),
            pltpu.VMEM((2, rows, width), bf16),
            pltpu.VMEM((3, 8, 128), f32),
            pltpu.VMEM((3, 3, 8, 128), f32),
            dma((3, 4)),
            dma,
            dma((3, 3)),
            dma((3, 3)),
            dma((31,)),
            dma((31,)),
            dma((31,)),
            dma((31,)),
            dma((31, 4)),
            dma((31, 4)),
            dma((31, 4)),
            dma((31, 4)),
            dma((4, 3)),
            dma((4, 3)),
            dma((4, 3)),
            dma((4, 3)),
            dma((3,)),
            dma((3,)),
            dma((2, 3)),
            dma((2, 3)),
        ],
        compiler_params=pltpu.CompilerParams(
            collective_id=1, has_side_effects=True, vmem_limit_bytes=VMEM_LIMIT
        ),
        name="main_part",
    )(query_hidden, passage_hidden, head_weight, neg_blocks, positions)


def local(query_hidden, passage_hidden, head_weight, neg_blocks, pos_ids):
    (
        losses,
        passage_norm,
        inverses,
        table,
        d_query,
        own_terms,
        returned,
        query_grad,
    ) = main_part(query_hidden, passage_hidden, head_weight, neg_blocks, pos_ids)
    block_sums = add_returned(table, returned.reshape(512, 16, 256))
    grad_weight, passage_grad = tail(
        d_query,
        block_sums,
        own_terms,
        passage_norm,
        inverses,
        query_hidden,
        passage_hidden,
        head_weight,
    )
    return losses.reshape(512), grad_weight, query_grad, passage_grad


def solution(mesh):
    placed = (P("dp", None), P("dp", None), P(None, "mp"), P("dp", None), P("dp"))
    return jax.shard_map(
        local,
        mesh=mesh,
        in_specs=placed,
        out_specs=(P("dp"), P("dp", "mp"), P("dp", "mp"), P("dp", "mp")),
        check_vma=False,
    )
```

```python
import jax
import jax.numpy as jnp
from jax import lax
from jax.experimental import pallas as pl
from jax.experimental.pallas import tpu as pltpu
from jax.sharding import PartitionSpec as P

logit_divisor = 0.02
epsilon = 1e-06


MESH = pl.DeviceIdType.MESH
ROW_CONTRACT = (((0,), (0,)), ((), ()))
COL_CONTRACT = (((1,), (1,)), ((), ()))
VMEM_LIMIT = 66 * 1024 * 1024 - 4 * 1024 * 1024


def greet(partners):
    barrier = pltpu.get_barrier_semaphore()
    for partner in partners:
        pl.semaphore_signal(barrier, 1, device_id=partner, device_id_type=MESH)
    pl.semaphore_wait(barrier, len(partners))


def remote(src, dst, send_sem, recv_sem, partner):
    return pltpu.make_async_remote_copy(
        src_ref=src,
        dst_ref=dst,
        send_sem=send_sem,
        recv_sem=recv_sem,
        device_id=partner,
        device_id_type=MESH,
    )


def depth_partner(k):
    return {"mp": lax.rem(lax.axis_index("mp") + k, 4)}


def head_load(head_hbm, head, load_sem, k):
    width = head.shape[1]
    owner = lax.rem(lax.axis_index("mp") + k, 4)
    return pltpu.make_async_copy(
        head_hbm.at[pl.ds(pl.multiple_of(owner * width, width), width)], head.at[k], load_sem.at[k]
    )


def hidden_send(part, early_in, final_in, send_sem, recv_sem, side, stage):
    half = part.shape[1] // 2
    merged_rows = pl.ds(side * half, half)
    plain_rows = pl.ds((1 - side) * half, half)
    near = (1, 3)[side]
    if stage == 0:
        src, dst = part.at[2, merged_rows], early_in.at[side]
    elif stage == 1:
        src, dst = part.at[near, plain_rows], final_in.at[side, plain_rows]
    else:
        src, dst = part.at[near, merged_rows], final_in.at[side, merged_rows]
    return remote(src, dst, send_sem.at[side, stage], recv_sem.at[side, stage], depth_partner(near))


DEPTH_ORDER = (2, 1, 3, 0)


def hidden_dot(grad, head, out):
    half = grad.shape[0] // 2

    @pl.loop(0, 2)
    def _(i):
        rows = pl.ds(pl.multiple_of(i * half, half), half)
        out[rows] = lax.dot_general(
            grad[rows], head[...], COL_CONTRACT, preferred_element_type=jnp.float32
        ).astype(jnp.bfloat16)


def hidden_parts(grad, head_of, part, early_in, final_in, send_sem, recv_sem):
    sends = (part, early_in, final_in, send_sem, recv_sem)
    for k in (2, 1, 3):
        hidden_dot(grad, head_of(k), part.at[k])
        if k == 2:
            hidden_send(*sends, 0, 0).start()
            hidden_send(*sends, 1, 0).start()
        else:
            hidden_send(*sends, k // 2, 1).start()


def hidden_merge(part, early_in, final_in, send_sem, recv_sem):
    half = part.shape[1] // 2
    step = 64
    for side in range(2):
        hidden_send(part, early_in, final_in, send_sem, recv_sem, side, 0).wait_recv()
        near = (1, 3)[side]

        @pl.loop(0, half // step)
        def _(i):
            rows = pl.ds(pl.multiple_of(side * half + i * step, step), step)
            early_rows = pl.ds(pl.multiple_of(i * step, step), step)
            part[near, rows] = (
                part[near, rows].astype(jnp.float32)
                + early_in[side, early_rows].astype(jnp.float32)
            ).astype(jnp.bfloat16)

        hidden_send(part, early_in, final_in, send_sem, recv_sem, side, 2).start()


def hidden_finish(*sends):
    for stage in (1, 2):
        for side in range(2):
            hidden_send(*sends, side, stage).wait_recv()
    for stage in range(3):
        for side in range(2):
            hidden_send(*sends, side, stage).wait_send()


def finish_kernel(
    near_a, landed_a, near_b, landed_b, near_p, landed_p, weight, query_out, passage_out, weight_out
):
    def total(near, landed):
        result = near[...].astype(jnp.float32) + landed[0].astype(jnp.float32)
        return (result + landed[1].astype(jnp.float32)).astype(jnp.bfloat16)

    early = pl.program_id(0) < 2

    @pl.when(early)
    def _():
        query_out[...] = total(near_a, landed_a)

    @pl.when(jnp.logical_not(early))
    def _():
        query_out[...] = total(near_b, landed_b)

    passage_out[...] = total(near_p, landed_p)
    weight_out[...] = weight[...]


def finish(near_a, landed_a, near_b, landed_b, near_p, landed_p, weight):
    rows, width = near_p.shape
    block = rows // 4
    share = weight.shape[0] // 4
    first = lambda i: jnp.minimum(i, 1)
    second = lambda i: jnp.maximum(i - 2, 0)
    same = lambda i: i

    def near(index):
        return pl.BlockSpec((block, width), lambda i: (index(i), 0))

    def landed(index):
        return pl.BlockSpec((2, block, width), lambda i: (0, index(i), 0))

    weight_spec = pl.BlockSpec((share, width), lambda i: (i, 0))
    return pl.pallas_call(
        finish_kernel,
        grid=(4,),
        out_shape=(
            jax.ShapeDtypeStruct((rows, width), jnp.bfloat16),
            jax.ShapeDtypeStruct((rows, width), jnp.bfloat16),
            jax.ShapeDtypeStruct(weight.shape, jnp.float32),
        ),
        in_specs=[
            near(first),
            landed(first),
            near(second),
            landed(second),
            near(same),
            landed(same),
            weight_spec,
        ],
        out_specs=(near(same), near(same), weight_spec),
        name="finish",
    )(near_a, landed_a, near_b, landed_b, near_p, landed_p, weight)


def place():
    dp = lax.axis_index("dp")
    return lax.div(dp, 8), lax.rem(lax.div(dp, 2), 4), lax.rem(dp, 2)


def at(y, x, core):
    return {"dp": y * 8 + x * 2 + core}


OFFSETS = tuple(
    (dy, dx, core)
    for dy, dx in (
        (2, 2), (1, 3), (3, 1), (1, 1), (3, 3), (0, 2), (2, 0), (1, 2),
        (3, 2), (2, 1), (2, 3), (0, 1), (1, 0), (0, 3), (3, 0), (0, 0),
    )
    for core in range(2)
    if dy or dx or core
)


def plane_peer(offset):
    y, x, core = place()
    return (
        lax.rem(y + offset[0], 4) * 8 + lax.rem(x + offset[1], 4) * 2 + lax.rem(core + offset[2], 2)
    )


def share_rows(device):
    return pl.ds(pl.multiple_of(lax.div(device, 4) * 16, 16), 16)


def share_cols(device):
    return pl.ds(pl.multiple_of(lax.rem(device, 4) * 256, 256), 256)


def diagonal():
    rows = lax.broadcasted_iota(jnp.int32, (128, 128), 0)
    return rows == lax.broadcasted_iota(jnp.int32, (128, 128), 1)


def as_row(column):
    spread = jnp.broadcast_to(column, (128, 128))
    return jnp.sum(jnp.where(diagonal(), spread, 0.0), axis=0, keepdims=True)


def as_column(row):
    spread = jnp.broadcast_to(row, (128, 128))
    return jnp.sum(jnp.where(diagonal(), spread, 0.0), axis=1, keepdims=True)


def depth_copy(src, dst, send_sem, recv_sem, k):
    return remote(src, dst.at[k - 1], send_sem.at[k - 1], recv_sem.at[k - 1], depth_partner(k))


def depth_start(src, dst, send_sem, recv_sem):
    for k in (2, 1, 3):
        depth_copy(src, dst, send_sem, recv_sem, k).start()


def depth_total(src, dst, send_sem, recv_sem):
    for k in (1, 3, 2):
        depth_copy(src, dst, send_sem, recv_sem, k).wait_recv()
    return src[...] + dst[0] + dst[1] + dst[2]


def depth_finish(src, dst, send_sem, recv_sem):
    for k in (1, 2, 3):
        depth_copy(src, dst, send_sem, recv_sem, k).wait_send()


def embed_grad(inverse_row, unit, d_unit, inner_row):
    return (
        as_column(inverse_row) * (d_unit - unit.astype(jnp.float32) * as_column(inner_row))
    ).astype(jnp.bfloat16)


def add_kernel(table, returned, out, total):
    total[...] = jnp.zeros_like(total)

    @pl.loop(0, 512, unroll=4)
    def _(i):
        block = table[i]
        total[block] += returned[i].astype(jnp.float32)

    out[...] = total[...].astype(jnp.bfloat16)


def add_returned(table, returned):
    vmem = pl.BlockSpec(memory_space=pltpu.VMEM)
    return pl.pallas_call(
        add_kernel,
        out_shape=jax.ShapeDtypeStruct((128, 16, 256), jnp.bfloat16),
        in_specs=[pl.BlockSpec(memory_space=pltpu.SMEM), vmem],
        out_specs=vmem,
        scratch_shapes=[pltpu.VMEM((128, 16, 256), jnp.float32)],
        name="add_returned",
    )(table, returned)


def tail_kernel(
    block_sums,
    inverses,
    d_query_hbm,
    own_hbm,
    norm_hbm,
    query_hbm,
    passage_hbm,
    head_hbm,
    weight_out,
    near_out,
    final_in,
    query_near_out,
    query_final_in,
    query_part,
    query_early_in,
    query_depth_send,
    query_depth_recv,
    d_query,
    passage_norm,
    home,
    d_total,
    extra_sem,
    d_passage,
    inner,
    inner_in,
    home_send,
    home_recv,
    inner_send,
    inner_recv,
    head,
    query,
    passage,
    summed,
    sibling_in,
    pair,
    first_in,
    second_out,
    second_in,
    part,
    early_in,
    load_sem,
    hidden_load_sem,
    depth_send,
    depth_recv,
    core_send,
    core_recv,
    first_send,
    first_recv,
    second_send,
    second_recv,
):
    y, x, core = place()
    wide = query.shape[1]
    rows = weight_out.shape[0]
    half = weight_out.shape[1] // 2

    def chunk_of(i):
        return lax.rem(y + 1 + lax.div(i, 2), 4) * 2 + lax.rem(lax.div(x, 2) + 1 + i, 2)

    def hidden_load(side, i, slot):
        columns = pl.ds(pl.multiple_of(chunk_of(i) * wide, wide), wide)
        source, buffer = ((query_hbm, query), (passage_hbm, passage))[side]
        return pltpu.make_async_copy(
            source.at[:, columns], buffer.at[slot], hidden_load_sem.at[side, slot]
        )

    for k in DEPTH_ORDER:
        head_load(head_hbm, head, load_sem, k).start()
    extra_loads = (
        pltpu.make_async_copy(d_query_hbm, d_query, extra_sem.at[0]),
        pltpu.make_async_copy(own_hbm, d_total, extra_sem.at[1]),
        pltpu.make_async_copy(norm_hbm, passage_norm, extra_sem.at[2]),
    )
    for copy in extra_loads:
        copy.start()
    for i in range(2):
        hidden_load(0, i, i).start()
    greet(
        [{"dp": plane_peer(offset)} for offset in OFFSETS]
        + [depth_partner(k) for k in (1, 2, 3)]
    )
    dp = lax.axis_index("dp")

    def home_copy(j):
        peer = plane_peer(OFFSETS[j])
        return remote(
            block_sums.at[pl.ds(peer * 4, 4)],
            home.at[:, share_rows(dp), share_cols(dp)],
            home_send.at[j],
            home_recv.at[j],
            {"dp": peer},
        )

    for j in range(31):
        home_copy(j).start()
    home[:, share_rows(dp), share_cols(dp)] = block_sums[pl.ds(dp * 4, 4)]
    inner[4:8] = jnp.zeros((4, 128), jnp.float32)
    for copy in extra_loads:
        copy.wait()
    for k in DEPTH_ORDER:
        head_load(head_hbm, head, load_sem, k).wait()
    query_args = (query_part, query_early_in, query_final_in, query_depth_send, query_depth_recv)
    second_half = d_query.at[query_near_out.shape[0] :]
    hidden_parts(second_half, lambda k: head.at[k], *query_args)
    hidden_dot(second_half, head.at[0], query_near_out)

    @pl.loop(0, 8)
    def _(i):
        slot = lax.rem(i, 2)
        hidden_load(0, i, slot).wait()
        chunk = chunk_of(i)
        for j in range(2):
            columns = slice(j * 2 * rows, (j + 1) * 2 * rows)
            total = lax.dot_general(
                query[slot, :, columns], d_query[...], ROW_CONTRACT, preferred_element_type=jnp.float32
            )
            summed[chunk * 2 + j] = total.astype(jnp.bfloat16).reshape(2, rows, 2 * half)

        @pl.when(i < 6)
        def _():
            hidden_load(0, i + 2, slot).start()

    for i in range(2):
        hidden_load(1, i, i).start()
    hidden_merge(*query_args)
    for j in range(31):
        home_copy(j).wait_recv()
    for b in range(4):
        total = d_total[b] + home[b].astype(jnp.float32)
        d_total[b] = total
        inner[b : b + 1] = as_row(
            jnp.sum(passage_norm[b].astype(jnp.float32) * total, axis=1, keepdims=True)
        )
    inner_args = (inner, inner_in, inner_send, inner_recv)
    depth_start(*inner_args)
    total_inner = depth_total(*inner_args)
    for b in range(4):
        d_passage[b * 128 : (b + 1) * 128] = embed_grad(
            inverses[0, b : b + 1], passage_norm[b], d_total[b], total_inner[b : b + 1]
        )
    depth_args = (part, early_in, final_in, depth_send, depth_recv)
    hidden_parts(d_passage, lambda k: head.at[k], *depth_args)

    def core_copy(chip):
        return remote(
            summed.at[chip, 1 - core],
            sibling_in.at[chip],
            core_send.at[chip],
            core_recv.at[chip],
            at(y, x, 1 - core),
        )

    def first_x(chip):
        to_y, to_x = lax.div(chip, 4), lax.rem(chip, 4)
        k = lax.rem(to_x - x + 4, 4)
        slot = lax.rem(k + 3, 4)
        return k, remote(
            pair.at[chip, 0],
            first_in.at[0, slot, to_y],
            first_send.at[0, chip],
            first_recv.at[0, slot, to_y],
            at(y, to_x, core),
        )

    def first_y(chip):
        to_y, to_x = lax.div(chip, 4), lax.rem(chip, 4)
        k = lax.rem(to_y - y + 4, 4)
        slot = lax.rem(k + 3, 4)
        return k, remote(
            pair.at[chip, 1],
            first_in.at[1, slot, to_x],
            first_send.at[1, chip],
            first_recv.at[1, slot, to_x],
            at(to_y, x, core),
        )

    def produce(i):
        slot = lax.rem(i, 2)
        hidden_load(1, i, slot).wait()
        chunk = chunk_of(i)
        for j in range(2):
            columns = slice(j * 2 * rows, (j + 1) * 2 * rows)
            chip = chunk * 2 + j
            total = lax.dot_general(
                passage[slot, :, columns],
                d_passage[...],
                ROW_CONTRACT,
                preferred_element_type=jnp.float32,
            ) + summed[chip].reshape(2 * rows, 2 * half).astype(jnp.float32)
            summed[chip] = total.astype(jnp.bfloat16).reshape(2, rows, 2 * half)
            core_copy(chunk * 2 + j).start()

        @pl.when(i < 6)
        def _():
            hidden_load(1, i + 2, slot).start()

    def combine(i):
        for j in range(2):
            chip = chunk_of(i) * 2 + j
            core_copy(chip).wait_recv()
            total = (
                summed[chip, core].astype(jnp.float32) + sibling_in[chip].astype(jnp.float32)
            ).astype(jnp.bfloat16)
            pair[chip, 0] = total[:, :half]
            pair[chip, 1] = total[:, half:]
            for first in (first_x, first_y):
                k, copy = first(chip)

                @pl.when(k != 0)
                def _():
                    copy.start()

    @pl.loop(0, 10)
    def _(i):
        @pl.when(i == 7)
        def _():
            hidden_merge(*depth_args)

        @pl.when(i < 8)
        def _():
            produce(i)

        @pl.when(i > 1)
        def _():
            combine(i - 2)

    hidden_dot(d_passage, head.at[0], near_out)

    def first_arrival(side, k, other):
        return remote(
            first_in.at[side, k, other],
            first_in.at[side, k, other],
            first_send.at[side, 0],
            first_recv.at[side, k, other],
            at(y, x, 1 - core),
        )

    def gathered(side, other):
        chip = other * 4 + x if side == 0 else y * 4 + other
        total = pair[chip, side].astype(jnp.float32)
        for k in range(3):
            first_arrival(side, k, other).wait_recv()
            total = total + first_in[side, k, other].astype(jnp.float32)
        return total

    def second_copy(side, k):
        if side == 0:
            partner = at(lax.rem(y + k, 4), x, core)
        else:
            partner = at(y, lax.rem(x + k, 4), core)
        return remote(
            second_out.at[side, k - 1],
            second_in.at[side, k - 1],
            second_send.at[side, k - 1],
            second_recv.at[side, k - 1],
            partner,
        )

    for k in (1, 2, 3):
        for side in range(2):
            base = y if side == 0 else x
            second_out[side, k - 1] = gathered(side, lax.rem(base + k, 4)).astype(jnp.bfloat16)
            second_copy(side, k).start()
    for side in range(2):
        weight_out[:, side * half : (side + 1) * half] = gathered(side, y if side == 0 else x)
    for side in range(2):
        for k in (1, 2, 3):
            second_copy(side, k).wait_recv()
            weight_out[:, side * half : (side + 1) * half] += second_in[side, k - 1].astype(
                jnp.float32
            )
    hidden_finish(*query_args)
    hidden_finish(*depth_args)
    for j in range(31):
        home_copy(j).wait_send()
    depth_finish(*inner_args)

    @pl.loop(0, 16)
    def _(chip):
        core_copy(chip).wait_send()
        for first in (first_x, first_y):
            k, copy = first(chip)

            @pl.when(k != 0)
            def _():
                copy.wait_send()

    for side in range(2):
        for k in (1, 2, 3):
            second_copy(side, k).wait_send()


def tail(
    d_query,
    block_sums,
    own_terms,
    passage_norm,
    inverses,
    query_hidden,
    passage_hidden,
    head_weight,
):
    rows, width = d_query.shape
    hidden = head_weight.shape[0]
    share = hidden // 32
    bf16 = jnp.bfloat16
    vmem = pl.BlockSpec(memory_space=pltpu.VMEM)
    hbm = pl.BlockSpec(memory_space=pl.ANY)
    dma = pltpu.SemaphoreType.DMA
    return pl.pallas_call(
        tail_kernel,
        out_shape=(
            jax.ShapeDtypeStruct((share, width), jnp.float32),
            jax.ShapeDtypeStruct((rows, width), bf16),
            jax.ShapeDtypeStruct((2, rows, width), bf16),
            jax.ShapeDtypeStruct((rows // 2, width), bf16),
            jax.ShapeDtypeStruct((2, rows // 2, width), bf16),
        ),
        in_specs=[vmem] * 2 + [hbm] * 6,
        out_specs=(vmem,) + (vmem, pl.BlockSpec(memory_space=pltpu.HBM)) * 2,
        scratch_shapes=[
            pltpu.VMEM((4, rows // 2, width), bf16),
            pltpu.VMEM((2, rows // 4, width), bf16),
            dma((2, 3)),
            dma((2, 3)),
            pltpu.VMEM((rows, width), bf16),
            pltpu.VMEM((4, 128, width), bf16),
            pltpu.VMEM((4, 128, width), bf16),
            pltpu.VMEM((4, 128, width), jnp.float32),
            dma((3,)),
            pltpu.VMEM((rows, width), bf16),
            pltpu.VMEM((8, 128), jnp.float32),
            pltpu.VMEM((3, 8, 128), jnp.float32),
            dma((31,)),
            dma((31,)),
            dma((3,)),
            dma((3,)),
            pltpu.VMEM((4, width, width), bf16),
            pltpu.VMEM((2, rows, 4 * share), bf16),
            pltpu.VMEM((2, rows, 4 * share), bf16),
            pltpu.VMEM((16, 2, share, width), bf16),
            pltpu.VMEM((16, share, width), bf16),
            pltpu.VMEM((16, 2, share, width // 2), bf16),
            pltpu.VMEM((2, 3, 4, share, width // 2), bf16),
            pltpu.VMEM((2, 3, share, width // 2), bf16),
            pltpu.VMEM((2, 3, share, width // 2), bf16),
            pltpu.VMEM((4, rows, width), bf16),
            pltpu.VMEM((2, rows // 2, width), bf16),
            dma((4,)),
            dma((2, 2)),
            dma((2, 3)),
            dma((2, 3)),
            dma((16,)),
            dma((16,)),
            dma((2, 16)),
            dma((2, 3, 4)),
            dma((2, 3)),
            dma((2, 3)),
        ],
        compiler_params=pltpu.CompilerParams(
            collective_id=2, has_side_effects=True, vmem_limit_bytes=VMEM_LIMIT
        ),
        name="tail",
    )(
        block_sums,
        inverses,
        d_query,
        own_terms,
        passage_norm,
        query_hidden,
        passage_hidden,
        head_weight,
    )


def main_kernel(
    query_hbm,
    passage_hbm,
    head_hbm,
    negatives,
    positions,
    losses,
    passage_norm,
    inverses,
    table,
    d_query_embed,
    own_terms,
    returned,
    near_out,
    final_in,
    head,
    hidden,
    embed,
    query_norm,
    wanted,
    all_wanted,
    wanted_smem,
    targets,
    held,
    reply,
    fetched,
    partial,
    partial_in,
    weights,
    loss_rows,
    outgoing,
    part,
    early_in,
    squares,
    squares_in,
    load_sem,
    table_sem,
    square_send,
    square_recv,
    want_send,
    want_recv,
    spread_send,
    spread_recv,
    reply_send,
    reply_recv,
    return_send,
    return_recv,
    partial_send,
    partial_recv,
    weight_send,
    weight_recv,
    loss_send,
    loss_recv,
    depth_send,
    depth_recv,
):
    dp = lax.axis_index("dp")
    mp = lax.axis_index("mp")
    depth = head.shape[1]
    hidden_hbm = (passage_hbm, query_hbm)
    my_rows = pl.ds(pl.multiple_of(mp * 32, 32), 32)

    def hidden_load(side, chunk):
        columns = pl.ds(pl.multiple_of(chunk * depth, depth), depth)
        return pltpu.make_async_copy(
            hidden_hbm[side].at[:, columns], hidden.at[side, chunk], load_sem.at[side, chunk]
        )

    def head_chunk(chunk):
        rows = pl.ds(pl.multiple_of(chunk * depth, depth), depth)
        return pltpu.make_async_copy(head_hbm.at[rows], head.at[chunk], load_sem.at[2, chunk])

    for chunk in range(4):
        hidden_load(0, chunk).start()
        head_chunk(chunk).start()
    for chunk in range(4):
        hidden_load(1, chunk).start()
    for i in range(16):
        wanted[i : i + 1] = jnp.full((1, 128), negatives[i // 4, i % 4], jnp.int32)
    embed[...] = jnp.zeros_like(embed)
    greet(
        [{"dp": plane_peer(offset)} for offset in OFFSETS]
        + [depth_partner(k) for k in (1, 2, 3)]
    )

    def want_copy(j):
        return remote(
            wanted,
            all_wanted.at[dp],
            want_send.at[j],
            want_recv.at[j],
            {"dp": plane_peer(OFFSETS[j])},
        )

    for j in range(31):
        want_copy(j).start()
    all_wanted[dp] = wanted[...]
    for b in range(4):
        row = positions[b * 128 : (b + 1) * 128].astype(jnp.float32).reshape(1, 128)
        targets[b] = jnp.broadcast_to(as_column(row), (128, 128))

    def project(side):
        @pl.loop(0, 4)
        def _(chunk):
            hidden_load(side, chunk).wait()
            if side == 0:
                head_chunk(chunk).wait()

            @pl.loop(0, 2)
            def _(i):
                rows = pl.ds(pl.multiple_of(i * 256, 256), 256)
                embed[side, rows] += jnp.dot(
                    hidden[side, chunk, rows], head[chunk], preferred_element_type=jnp.float32
                )

        for b in range(4):
            block = embed[side, b * 128 : (b + 1) * 128]
            squares[side, b : b + 1] = as_row(jnp.sum(block * block, axis=1, keepdims=True))
        squares[side, 4:8] = jnp.zeros((4, 128), jnp.float32)

    def square_args(side):
        return squares.at[side], squares_in.at[side], square_send.at[side], square_recv.at[side]

    def normalize(side, out):
        inverses[side] = lax.rsqrt(depth_total(*square_args(side)) + epsilon)
        for b in range(4):
            inverse = as_column(inverses[side, b : b + 1])
            out[b] = (embed[side, b * 128 : (b + 1) * 128] * inverse).astype(jnp.bfloat16)

    project(0)
    depth_start(*square_args(0))
    normalize(0, passage_norm)

    def spread_copy(j):
        peer = plane_peer(OFFSETS[j])
        return remote(
            passage_norm.at[:, share_rows(peer), share_cols(peer)],
            held.at[pl.ds(dp * 4, 4)],
            spread_send.at[j],
            spread_recv.at[j],
            {"dp": peer},
        )

    for j in range(31):
        spread_copy(j).start()
    for b in range(4):
        held[dp * 4 + b] = passage_norm[b, share_rows(dp), share_cols(dp)]
    project(1)
    depth_start(*square_args(1))
    normalize(1, query_norm)
    for j in range(31):
        want_copy(j).wait_recv()
    table_copy = pltpu.make_async_copy(all_wanted, wanted_smem, table_sem)
    table_copy.start()
    table_copy.wait()
    for j in range(31):
        spread_copy(j).wait_recv()

    def four(b):
        return pl.ds(b * 4, 4)

    def reply_copy(j, b):
        peer = plane_peer(OFFSETS[j])
        return remote(
            reply.at[peer, four(b)],
            fetched.at[four(b), share_rows(dp), share_cols(dp)],
            reply_send.at[j, b],
            reply_recv.at[j, b],
            {"dp": peer},
        )

    def gather(device, b):
        for i in range(4):
            reply[device, b * 4 + i] = held[wanted_smem[device, b * 4 + i, 0]]

    @pl.loop(0, 4)
    def _(b):
        for j in range(31):
            gather(plane_peer(OFFSETS[j]), b)
            reply_copy(j, b).start()
        gather(dp, b)
        fetched[four(b), share_rows(dp), share_cols(dp)] = reply[dp, four(b)]

    @pl.loop(0, 32)
    def _(device):
        for i in range(16):
            table[device * 16 + i] = wanted_smem[device, i, 0]

    def partial_copy(b, k):
        peer_rows = pl.ds(pl.multiple_of(lax.rem(mp + k, 4) * 32, 32), 32)
        return depth_copy(
            partial.at[b, peer_rows], partial_in.at[b], partial_send.at[b], partial_recv.at[b], k
        )

    def score(b):
        for j in range(31):
            reply_copy(j, b).wait_recv()
        rows = query_norm[b]
        partial[b, :, :128] = lax.dot_general(
            rows, passage_norm[b], COL_CONTRACT, preferred_element_type=jnp.float32
        ).astype(jnp.bfloat16)
        others = fetched[four(b)].reshape(512, depth)
        partial[b, :, 128:] = lax.dot_general(
            rows, others, COL_CONTRACT, preferred_element_type=jnp.float32
        ).astype(jnp.bfloat16)
        for k in (2, 1, 3):
            partial_copy(b, k).start()

    def weight_copy(b, k):
        return remote(
            weights.at[b, my_rows],
            weights.at[b, my_rows],
            weight_send.at[b, k - 1],
            weight_recv.at[b, k - 1],
            depth_partner(k),
        )

    def weigh(b):
        scores = partial[b, my_rows].astype(jnp.float32)
        for k in (1, 3, 2):
            partial_copy(b, k).wait_recv()
            scores = scores + partial_in[b, k - 1].astype(jnp.float32)
        scores = scores / logit_divisor
        columns = lax.broadcasted_iota(jnp.int32, scores.shape, 1).astype(jnp.float32)
        matching = (columns == targets[b, my_rows][:, :1]).astype(jnp.float32)
        powers = jnp.exp(scores)
        totals = jnp.sum(powers, axis=1, keepdims=True)
        loss = jnp.log(totals) - jnp.sum(scores * matching, axis=1, keepdims=True)
        weights[b, my_rows] = ((powers / totals - matching) / logit_divisor).astype(jnp.bfloat16)
        loss_rows[b, my_rows] = jnp.broadcast_to(loss, (32, 128))
        for k in (2, 1, 3):
            weight_copy(b, k).start()

    def return_copy(j, b):
        peer = plane_peer(OFFSETS[j])
        return remote(
            outgoing.at[four(b), share_rows(peer), share_cols(peer)],
            returned.at[dp, four(b)],
            return_send.at[j, b],
            return_recv.at[j, b],
            {"dp": peer},
        )

    def give_back(b):
        for k in (1, 3, 2):
            weight_copy(b, k).wait_recv()
        outgoing[four(b)] = (
            lax.dot_general(
                weights[b, :, 128:],
                query_norm[b],
                ROW_CONTRACT,
                preferred_element_type=jnp.float32,
            )
            .astype(jnp.bfloat16)
            .reshape(4, 128, depth)
        )
        for j in range(31):
            return_copy(j, b).start()
        returned[dp, four(b)] = outgoing[four(b), share_rows(dp), share_cols(dp)]
        total = jnp.dot(
            weights[b, :, :128], passage_norm[b], preferred_element_type=jnp.float32
        ) + jnp.dot(
            weights[b, :, 128:],
            fetched[four(b)].reshape(512, depth),
            preferred_element_type=jnp.float32,
        )
        embed[0, pl.ds(pl.multiple_of(b * 128, 128), 128)] = total
        squares[2, pl.ds(b, 1)] = as_row(
            jnp.sum(query_norm[b].astype(jnp.float32) * total, axis=1, keepdims=True)
        )
        own_terms[b] = lax.dot_general(
            weights[b, :, :128], query_norm[b], ROW_CONTRACT, preferred_element_type=jnp.float32
        )

    squares[2, 4:8] = jnp.zeros((4, 128), jnp.float32)

    @pl.loop(0, 6)
    def _(step):
        @pl.when(step < 4)
        def _():
            score(step)

        @pl.when((step >= 1) & (step < 5))
        def _():
            weigh(step - 1)

        @pl.when(step >= 2)
        def _():
            give_back(step - 2)

    depth_start(*square_args(2))

    def loss_copy(k):
        return remote(
            loss_rows.at[:, my_rows],
            loss_rows.at[:, my_rows],
            loss_send.at[k - 1],
            loss_recv.at[k - 1],
            depth_partner(k),
        )

    for k in (2, 1, 3):
        loss_copy(k).start()
    inner = depth_total(*square_args(2))
    for b in range(4):
        d_query_embed[b * 128 : (b + 1) * 128] = embed_grad(
            inverses[1, b : b + 1],
            query_norm[b],
            embed[0, b * 128 : (b + 1) * 128],
            inner[b : b + 1],
        )
    depth_args = (part, early_in, final_in, depth_send, depth_recv)
    first_half = d_query_embed.at[: near_out.shape[0]]
    hidden_parts(first_half, lambda k: head.at[lax.rem(mp + k, 4)], *depth_args)
    hidden_dot(first_half, head.at[mp], near_out)
    for k in (1, 3, 2):
        loss_copy(k).wait_recv()
    for b in range(4):
        losses[b : b + 1] = as_row(loss_rows[b, :, :1])
    hidden_merge(*depth_args)
    for j in range(31):
        want_copy(j).wait_send()
        spread_copy(j).wait_send()
    for side in range(3):
        depth_finish(*square_args(side))
    for k in (1, 2, 3):
        loss_copy(k).wait_send()

    @pl.loop(0, 4)
    def _(b):
        for k in (1, 2, 3):
            partial_copy(b, k).wait_send()
            weight_copy(b, k).wait_send()
        for j in range(31):
            reply_copy(j, b).wait_send()
            return_copy(j, b).wait_send()
            return_copy(j, b).wait_recv()

    hidden_finish(*depth_args)


def main_part(query_hidden, passage_hidden, head_weight, neg_blocks, pos_ids):
    bf16 = jnp.bfloat16
    f32 = jnp.float32
    rows = query_hidden.shape[0]
    width = head_weight.shape[1]
    vmem = pl.BlockSpec(memory_space=pltpu.VMEM)
    smem = pl.BlockSpec(memory_space=pltpu.SMEM)
    hbm = pl.BlockSpec(memory_space=pl.ANY)
    dma = pltpu.SemaphoreType.DMA
    return pl.pallas_call(
        main_kernel,
        out_shape=(
            jax.ShapeDtypeStruct((4, 128), f32),
            jax.ShapeDtypeStruct((4, 128, width), bf16),
            jax.ShapeDtypeStruct((2, 8, 128), f32),
            jax.ShapeDtypeStruct((512,), jnp.int32),
            jax.ShapeDtypeStruct((rows, width), bf16),
            jax.ShapeDtypeStruct((4, 128, width), f32),
            jax.ShapeDtypeStruct((32, 16, 16, 256), bf16),
            jax.ShapeDtypeStruct((rows // 2, width), bf16),
            jax.ShapeDtypeStruct((2, rows // 2, width), bf16),
        ),
        in_specs=[hbm, hbm, hbm, smem, vmem],
        out_specs=(vmem, vmem, vmem, smem, vmem, vmem, vmem, vmem)
        + (pl.BlockSpec(memory_space=pltpu.HBM),),
        scratch_shapes=[
            pltpu.VMEM((4, width, width), bf16),
            pltpu.VMEM((2, 4, rows, width), bf16),
            pltpu.VMEM((2, rows, width), f32),
            pltpu.VMEM((4, 128, width), bf16),
            pltpu.VMEM((16, 128), jnp.int32),
            pltpu.VMEM((32, 16, 128), jnp.int32),
            pltpu.SMEM((32, 16, 128), jnp.int32),
            pltpu.VMEM((4, 128, 128), f32),
            pltpu.VMEM((128, 16, 256), bf16),
            pltpu.VMEM((32, 16, 16, 256), bf16),
            pltpu.VMEM((16, 128, width), bf16),
            pltpu.VMEM((4, 128, 640), bf16),
            pltpu.VMEM((4, 3, 32, 640), bf16),
            pltpu.VMEM((4, 128, 640), bf16),
            pltpu.VMEM((4, 128, 128), f32),
            pltpu.VMEM((16, 128, width), bf16),
            pltpu.VMEM((4, rows // 2, width), bf16),
            pltpu.VMEM((2, rows // 4, width), bf16),
            pltpu.VMEM((3, 8, 128), f32),
            pltpu.VMEM((3, 3, 8, 128), f32),
            dma((3, 4)),
            dma,
            dma((3, 3)),
            dma((3, 3)),
            dma((31,)),
            dma((31,)),
            dma((31,)),
            dma((31,)),
            dma((31, 4)),
            dma((31, 4)),
            dma((31, 4)),
            dma((31, 4)),
            dma((4, 3)),
            dma((4, 3)),
            dma((4, 3)),
            dma((4, 3)),
            dma((3,)),
            dma((3,)),
            dma((2, 3)),
            dma((2, 3)),
        ],
        compiler_params=pltpu.CompilerParams(
            collective_id=1, has_side_effects=True, vmem_limit_bytes=VMEM_LIMIT
        ),
        name="main_part",
    )(query_hidden, passage_hidden, head_weight, neg_blocks, pos_ids)


def local(query_hidden, passage_hidden, head_weight, neg_blocks, pos_ids):
    (
        losses,
        passage_norm,
        inverses,
        table,
        d_query,
        own_terms,
        returned,
        near_a,
        landed_a,
    ) = main_part(query_hidden, passage_hidden, head_weight, neg_blocks, pos_ids)
    block_sums = add_returned(table, returned.reshape(512, 16, 256))
    weight, near_p, landed_p, near_b, landed_b = tail(
        d_query,
        block_sums,
        own_terms,
        passage_norm,
        inverses,
        query_hidden,
        passage_hidden,
        head_weight,
    )
    query_grad, passage_grad, grad_weight = finish(
        near_a, landed_a, near_b, landed_b, near_p, landed_p, weight
    )
    return losses.reshape(512), grad_weight, query_grad, passage_grad


def solution(mesh):
    placed = (P("dp", None), P("dp", None), P(None, "mp"), P("dp", None), P("dp"))
    return jax.shard_map(
        local,
        mesh=mesh,
        in_specs=placed,
        out_specs=(P("dp"), P("dp", "mp"), P("dp", "mp"), P("dp", "mp")),
        check_vma=False,
    )
```
